128 devices in a mesh: dp: 2 (over x_lo), ctx: 16 (over z, x_hi, core), space: 4 (over y).
Axes of the slice: x: 4 (x_hi: 2, x_lo: 2; x = x_hi * 2 + x_lo), y: 4, z: 4, core: 2. Of those that a mesh axis runs over, the one named last changes fastest.
Arguments:
- inputs: bfloat16 [8, 16, 256, 3072], P('dp', 'ctx', 'space'), may hold values from -64 to 64
- upstream: bfloat16 [8, 16, 256, 3072], P('dp', 'ctx', 'space'), may hold values from -6 to 6
- qkv_weight: bfloat16 [3, 3072, 1536], P(None, None, 'space'), may hold values from -0.109375 to 0.109375
- out_weight: bfloat16 [3072, 1536], P(None, 'space'), may hold values from -0.15625 to 0.15625
Outputs:
- input_grad: bfloat16 [8, 16, 256, 3072], P('dp', 'ctx', 'space')
- qkv_grad: float32 [3, 3072, 1536], P(None, ('dp', 'ctx'), 'space')
- proj_grad: float32 [3072, 1536], P(('dp', 'ctx'), 'space')
The draws below stay inside these ranges and needn't reach their ends.
All inputs are finite; a program needn't handle non-finite values.
Results may differ from the reference program's by a relative error of at most 0.01.
The reference program's roundings to bfloat16 on the way count: a program that leaves them out, or rounds other values in their place, can miss the bound.
Values may be sent and summed in bfloat16 or wider, within the bound.
A program may use at most 192 MiB of HBM per device.

```python
import math
import jax
import jax.numpy as jnp
from jax import lax

D = 3072
HEADS = 12
HS = 128
CLIPS = 8
FRAMES = 16
PATCHES = 256
E = 1536
N_SPACE = 4


def draw_inputs(key, part):
    key_base = jax.random.fold_in(jax.random.fold_in(key, 17), 0)
    shape = (CLIPS, FRAMES, PATCHES, D)
    values = jnp.clip(jax.random.normal(key_base, shape, jnp.float32), -6.0, 6.0)
    return jnp.clip(values, -64.0, 64.0).astype(jnp.bfloat16)


def spiked(values, rng, source, target, shards_of, factor):
    owner, partner = [(jnp.arange(values.shape[position]) // (values.shape[position] // shards_of)).reshape([-1 if axis == position else 1 for axis in range(values.ndim)]) for position in (source, target)]
    chosen = jax.random.permutation(rng, shards_of)[partner]
    strong = (owner == chosen) | (owner == (partner + shards_of // 2) % shards_of)
    return jnp.where(strong, factor * values, values)


def block_levels(stream_key, extent, pieces, low, high):
    level, own = 1.0, jax.random.fold_in(stream_key, 6)
    for position, parts in pieces:
        steps = jnp.exp(jax.random.uniform(jax.random.fold_in(own, position), (parts,), jnp.float32, low / len(pieces), high / len(pieces)))
        level = level * jnp.repeat(steps, extent[position] // parts).reshape([-1 if axis == position else 1 for axis in range(len(extent))])
    return level


def gaussian(key, shape, scale, most, cuts=(), dtype=jnp.bfloat16):
    level = block_levels(key, shape, cuts, -0.22, 0.18) if cuts else 1.0
    values = jax.random.normal(key, shape, jnp.float32) * scale * level
    return jnp.minimum(jnp.maximum(values, -most), most).astype(dtype)


def noise_with(own_key, extent, deviation, most, pieces, heavy, held_as=jnp.bfloat16):
    result = deviation * jax.random.normal(own_key, extent, jnp.float32)
    if pieces:
        result = result * block_levels(own_key, extent, pieces, -0.22, 0.18)
    return jnp.clip(spiked(result, jax.random.fold_in(own_key, 3), *heavy), -most, most).astype(held_as)


def setup_inputs(seed: int = 0) -> dict:
    key_of = jax.random.split(jax.random.key(seed), 5)
    return {
        "inputs": draw_inputs(jax.random.fold_in(key_of[4], 71), 0),
        "upstream": noise_with(key_of[1], (CLIPS, FRAMES, PATCHES, D), 1.0, 6.0, ((0, 2), (1, 16), (2, 4)), (1, 3, 16, 2.0)),
        "qkv_weight": gaussian(key_of[2], (3, D, E), D ** -0.5, 0.109375, ((2, 4),)),
        "out_weight": gaussian(key_of[3], (D, E), E ** -0.5, 0.15625, ((1, 4),)),
    }


def attend_clip(queries, key_rows, value_rows, out_front):
    frames = queries.shape[0]
    scale = 1.0 / math.sqrt(HS)

    def heads_view(array):
        return array.reshape(frames, array.shape[1], HEADS, HS).astype(jnp.float32)
    query_f = heads_view(queries)
    key_f = heads_view(key_rows)
    value_f = heads_view(value_rows)
    front_f = heads_view(out_front)
    scores = jnp.einsum('fphd,gphd->phfg', query_f, key_f) * scale
    causal = jnp.arange(frames)[:, None] >= jnp.arange(frames)[None, :]
    masked = jnp.where(causal, scores, jnp.float32(-1e+30))
    top = lax.optimization_barrier(jnp.max(masked, axis=-1, keepdims=True))
    expo = jnp.where(causal, jnp.exp(masked - top), jnp.float32(0.0))
    probs = expo / lax.optimization_barrier(jnp.sum(expo, axis=-1, keepdims=True))
    probs_b = probs.astype(jnp.bfloat16).astype(jnp.float32)
    attended = jnp.einsum('phfg,gphd->fphd', probs_b, value_f).astype(jnp.bfloat16)
    dprobs = jnp.einsum('fphd,gphd->phfg', front_f, value_f)
    dvalue = jnp.einsum('phfg,fphd->gphd', probs_b, front_f).astype(jnp.bfloat16)
    dscore = probs * (dprobs - lax.optimization_barrier(jnp.sum(probs * dprobs, axis=-1, keepdims=True)))
    dscore_b = dscore.astype(jnp.bfloat16).astype(jnp.float32)
    dquery = (jnp.einsum('phfg,gphd->fphd', dscore_b, key_f) * scale).astype(jnp.bfloat16)
    dkey = (jnp.einsum('phfg,fphd->gphd', dscore_b, query_f) * scale).astype(jnp.bfloat16)
    width = HEADS * HS
    shape = (frames, queries.shape[1], width)
    return (attended.reshape(shape), dquery.reshape(shape), dkey.reshape(shape), dvalue.reshape(shape))

def reference(inputs, upstream, qkv_weight, out_weight):
    width = HEADS * HS
    group = width // N_SPACE

    def one_clip(carry, pair):
        qkv_acc, proj_acc = carry
        clip_in, clip_up = pair
        frames, patches, model = clip_in.shape
        rows = clip_in.reshape(frames * patches, model)
        up_rows = clip_up.reshape(frames * patches, model)
        projected = [jnp.dot(rows, qkv_weight[s], preferred_element_type=jnp.float32).astype(jnp.bfloat16).reshape(frames, patches, width) for s in range(3)]
        out_front = jnp.dot(up_rows, out_weight, preferred_element_type=jnp.float32).astype(jnp.bfloat16).reshape(frames, patches, width)
        attended, dquery, dkey, dvalue = attend_clip(projected[0], projected[1], projected[2], out_front)
        grads = [dquery.reshape(-1, width), dkey.reshape(-1, width), dvalue.reshape(-1, width)]
        proj_acc = proj_acc + jnp.dot(up_rows.T, attended.reshape(-1, width), preferred_element_type=jnp.float32)
        qkv_acc = qkv_acc + jnp.stack([jnp.dot(rows.T, grads[s], preferred_element_type=jnp.float32) for s in range(3)])
        partial_value = jnp.zeros((N_SPACE, frames * patches, model), jnp.float32)
        for s in range(3):
            grad_g = grads[s].reshape(-1, N_SPACE, group).astype(jnp.float32)
            weight_g = qkv_weight[s].reshape(model, N_SPACE, group).astype(jnp.float32)
            partial_value = partial_value + jnp.einsum('tne,dne->ntd', grad_g, weight_g)
        rounded = lax.optimization_barrier(partial_value.astype(jnp.bfloat16)).astype(jnp.float32)
        clip_grad = lax.optimization_barrier(jnp.sum(rounded, axis=0)).astype(jnp.bfloat16).reshape(frames, patches, model)
        return ((qkv_acc, proj_acc), clip_grad)
    start = (jnp.zeros((3, D, width), jnp.float32), jnp.zeros((D, width), jnp.float32))
    (qkv_grad, proj_grad), input_grad = lax.scan(one_clip, start, (inputs, upstream))
    return (input_grad, qkv_grad, proj_grad)
```

```python
import math

import jax
import jax.numpy as jnp
from jax import lax
from jax.experimental import pallas as pl
from jax.experimental.pallas import tpu as pltpu
from jax.sharding import PartitionSpec as P


HS = 128
F32 = jnp.float32
BF16 = jnp.bfloat16


def nn(a, b):
    return lax.dot_general(a, b, (((1,), (0,)), ((), ())), preferred_element_type=F32)


def nt(a, b):
    return lax.dot_general(a, b, (((1,), (1,)), ((), ())), preferred_element_type=F32)


def tn(a, b):
    return lax.dot_general(a, b, (((0,), (0,)), ((), ())), preferred_element_type=F32)


def attend_kernel(pairs, width, qkv_ref, front_ref, att_ref, dqkv_ref):
    tokens = qkv_ref.shape[0]
    scale = 1.0 / math.sqrt(HS)
    row = lax.broadcasted_iota(jnp.int32, (tokens, tokens), 0)
    col = lax.broadcasted_iota(jnp.int32, (tokens, tokens), 1)
    valid = (row >= col) & (row % pairs == col % pairs)
    for head in range(width // HS):
        cols = slice(head * HS, (head + 1) * HS)
        k_cols = slice(width + head * HS, width + (head + 1) * HS)
        v_cols = slice(2 * width + head * HS, 2 * width + (head + 1) * HS)
        query, key, value = qkv_ref[:, cols], qkv_ref[:, k_cols], qkv_ref[:, v_cols]
        front = front_ref[:, cols]
        masked = jnp.where(valid, nt(query, key) * scale, F32(-1e30))
        top = jnp.max(masked, axis=-1, keepdims=True)
        expo = jnp.where(valid, jnp.exp(masked - top), F32(0.0))
        probs = expo / jnp.sum(expo, axis=-1, keepdims=True)
        probs_b = probs.astype(BF16)
        att_ref[:, cols] = nn(probs_b, value).astype(BF16)
        dprobs = nt(front, value)
        dqkv_ref[:, v_cols] = tn(probs_b, front).astype(BF16)
        weighed = probs * dprobs
        dscore = probs * (dprobs - jnp.sum(weighed, axis=-1, keepdims=True))
        dscore_b = dscore.astype(BF16)
        dqkv_ref[:, cols] = (nn(dscore_b, key) * scale).astype(BF16)
        dqkv_ref[:, k_cols] = (tn(dscore_b, query) * scale).astype(BF16)


def attend(qkv, front, pairs):
    tokens, width = front.shape
    return pl.pallas_call(
        lambda *refs: attend_kernel(pairs, width, *refs),
        out_shape=(
            jax.ShapeDtypeStruct((tokens, width), BF16),
            jax.ShapeDtypeStruct((tokens, 3 * width), BF16),
        ),
        in_specs=[pl.BlockSpec(memory_space=pltpu.VMEM)] * 2,
        out_specs=(pl.BlockSpec(memory_space=pltpu.VMEM),) * 2,
        cost_estimate=pl.CostEstimate(
            flops=7 * 2 * tokens * tokens * width,
            bytes_accessed=16 * tokens * width,
            transcendentals=tokens * tokens * width // HS,
        ),
        name="attend",
    )(qkv, front)


def grads_kernel(terms, rows, place_ref, *refs):
    n_in = 2 * sum(len(t) for t in terms)
    send_ref, keep_ref = refs[n_in], refs[n_in + 1]
    step = pl.program_id(0)
    x, core = place_ref[0], place_ref[2]
    first = lax.rem(step // 4 - x + 4, 4)
    at = 0
    low = 0
    for term in terms:
        total = None
        for _ in term:
            part = tn(refs[at][...], refs[at + 1][...])
            total = part if total is None else total + part
            at += 2
        high = low + total.shape[1]
        for hi in range(2):
            spot = lax.rem(first // 2 + hi, 2)
            even = total[2 * hi * rows : (2 * hi + 1) * rows]
            odd = total[(2 * hi + 1) * rows : (2 * hi + 2) * rows]
            send_ref[spot, 0, 0, :, low:high] = jnp.where(core == 0, odd, even)
            keep_ref[spot, 0, 0, :, low:high] = jnp.where(core == 0, even, odd)
        low = high


def grads(place, terms, rows):
    operands, specs, shapes = [], [], []
    width = 0
    flops = 0
    for term in terms:
        for source, grad, block, columns in term:
            tokens = source.shape[0]
            operands += [source, grad]
            specs += [
                pl.BlockSpec((tokens, 4 * rows), lambda i, place: (0, i)),
                pl.BlockSpec((tokens, columns), lambda i, place, block=block: (0, block)),
            ]
            flops += 2 * tokens * source.shape[1] * columns
        width += term[0][3]

    def out_map(i, place):
        first = lax.rem(i // 4 - place[0] + 4, 4)
        return (0, lax.rem(first, 2), lax.rem(lax.rem(i, 4) - place[1] + 4, 4), 0, 0)

    shape = jax.ShapeDtypeStruct((2, 2, 4, rows, width), F32)
    return pl.pallas_call(
        lambda *refs: grads_kernel(terms, rows, *refs),
        out_shape=(shape, shape),
        grid_spec=pltpu.PrefetchScalarGridSpec(
            num_scalar_prefetch=1,
            grid=(8,),
            in_specs=specs,
            out_specs=(pl.BlockSpec((2, 1, 1, rows, width), out_map),) * 2,
        ),
        cost_estimate=pl.CostEstimate(
            flops=flops, bytes_accessed=2 * 16 * rows * width * 4, transcendentals=0
        ),
        name="grads",
    )(place, *operands)


def solution(mesh):
    n_dp, n_ctx, n_space = mesh.shape["dp"], mesh.shape["ctx"], mesh.shape["space"]
    flat = ("dp", "ctx")

    def space_shift(array, by):
        return lax.ppermute(
            array, "space", [(i, (i + by) % n_space) for i in range(n_space)]
        )

    def spot(dp, ctx):
        return (ctx // 2 % 2) * 2 + dp, ctx // 4, ctx % 2

    def index(x, z, core):
        return (x % 2) * n_ctx + (z * 2 + x // 2) * 2 + core

    def plane(array, move):
        pairs = []
        for dp in range(n_dp):
            for ctx in range(n_ctx):
                x, z, core = move(*spot(dp, ctx))
                pairs.append((dp * n_ctx + ctx, index(x % 4, z % 4, core)))
        return lax.ppermute(array, flat, pairs)

    def x_shift(array, by):
        return plane(array, lambda x, z, core: (x + by, z, core))

    def z_shift(array, by):
        return plane(array, lambda x, z, core: (x, z + by, core))

    def core_swap(array):
        return plane(array, lambda x, z, core: (x, z, 1 - core))

    def spread(pieces, shift):
        got = [shift(pieces[d], d) for d in (2, 1, 3)]
        return pieces[0] + got[0] + got[1] + got[2]

    def body(inputs, upstream, qkv_weight, out_weight):
        clips, single, patches, model = inputs.shape
        width = out_weight.shape[1]
        pairs = clips * patches // n_ctx
        tokens = n_ctx * pairs
        dp, ctx = lax.axis_index("dp"), lax.axis_index("ctx")
        x, z, core = spot(dp, ctx)
        place = jnp.stack([x, z, core]).astype(jnp.int32)
        weight = jnp.transpose(qkv_weight, (1, 0, 2)).reshape(model, 3 * width)

        def to_frames(array):
            array = array.reshape(n_ctx, pairs, model)
            array = lax.all_to_all(array, "ctx", 0, 0, tiled=True)
            return array.reshape(tokens, model)

        def gather(own):
            behind, ahead = space_shift(own, 1), space_shift(own, -1)
            half = tokens // 2
            across = jnp.concatenate(
                [space_shift(behind[:half], 1), space_shift(ahead[half:], -1)]
            )
            return [own, behind, ahead, across]

        sources = gather(to_frames(inputs))
        up_sources = gather(to_frames(upstream))
        attended, gradients, parts = [], [], []
        for source, up_source in zip(sources, up_sources):
            qkv = nn(source, weight).astype(BF16)
            front = nn(up_source, out_weight).astype(BF16)
            att, dqkv = attend(qkv, front, pairs)
            attended.append(att)
            gradients.append(dqkv)
            parts.append(nt(dqkv, weight).astype(BF16))

        rows = model // (n_dp * n_ctx)
        units = range(4)
        send_a, keep_a = grads(
            place, [[(sources[u], gradients[u], 0, 2 * width) for u in units]], rows
        )
        got_a = core_swap(send_a)
        send_b, keep_b = grads(
            place,
            [
                [(sources[u], gradients[u], 2, width) for u in units],
                [(up_sources[u], attended[u], 0, width) for u in units],
            ],
            rows,
        )
        got_b = core_swap(send_b)
        sum_a = spread([keep_a[d // 2, d % 2] + got_a[d // 2, d % 2] for d in range(4)], x_shift)
        sum_a = spread([sum_a[d] for d in range(4)], z_shift)
        sum_b = spread([keep_b[:, :, d] + got_b[:, :, d] for d in range(4)], z_shift)
        sum_b = spread([sum_b[d // 2, d % 2] for d in range(4)], x_shift)
        qkv_grad = jnp.stack([sum_a[:, :width], sum_a[:, width:], sum_b[:, :width]])
        proj_grad = sum_b[:, width:]

        back = [
            parts[0],
            space_shift(parts[1], -1),
            space_shift(parts[2], 1),
            space_shift(parts[3], 2),
        ]
        total = sum(part.astype(F32) for part in back).astype(BF16)
        total = lax.all_to_all(total.reshape(n_ctx, pairs, model), "ctx", 0, 0, tiled=True)
        return total.reshape(clips, single, patches, model), qkv_grad, proj_grad

    placed = (
        P("dp", "ctx", "space", None),
        P("dp", "ctx", "space", None),
        P(None, None, "space"),
        P(None, "space"),
    )
    return jax.shard_map(
        body,
        mesh=mesh,
        in_specs=placed,
        out_specs=(
            P("dp", "ctx", "space", None),
            P(None, ("dp", "ctx"), "space"),
            P(("dp", "ctx"), "space"),
        ),
        check_vma=False,
    )
```

```python
import math

import jax
import jax.numpy as jnp
from jax import lax
from jax.experimental import pallas as pl
from jax.experimental.pallas import tpu as pltpu
from jax.sharding import PartitionSpec as P


HS = 128
F32 = jnp.float32
BF16 = jnp.bfloat16


def nn(a, b):
    return lax.dot_general(a, b, (((1,), (0,)), ((), ())), preferred_element_type=F32)


def nt(a, b):
    return lax.dot_general(a, b, (((1,), (1,)), ((), ())), preferred_element_type=F32)


def tn(a, b):
    return lax.dot_general(a, b, (((0,), (0,)), ((), ())), preferred_element_type=F32)


def attend_kernel(pairs, width, qkv_ref, front_ref, att_ref, dqkv_ref):
    tokens = qkv_ref.shape[0]
    scale = 1.0 / math.sqrt(HS)
    row = lax.broadcasted_iota(jnp.int32, (tokens, tokens), 0)
    col = lax.broadcasted_iota(jnp.int32, (tokens, tokens), 1)
    valid = (row >= col) & (row % pairs == col % pairs)
    for head in range(width // HS):
        cols = slice(head * HS, (head + 1) * HS)
        k_cols = slice(width + head * HS, width + (head + 1) * HS)
        v_cols = slice(2 * width + head * HS, 2 * width + (head + 1) * HS)
        query, key, value = qkv_ref[:, cols], qkv_ref[:, k_cols], qkv_ref[:, v_cols]
        front = front_ref[:, cols]
        masked = jnp.where(valid, nt(query, key) * scale, F32(-1e30))
        top = jnp.max(masked, axis=-1, keepdims=True)
        expo = jnp.where(valid, jnp.exp(masked - top), F32(0.0))
        probs = expo / jnp.sum(expo, axis=-1, keepdims=True)
        probs_b = probs.astype(BF16)
        att_ref[:, cols] = nn(probs_b, value).astype(BF16)
        dprobs = nt(front, value)
        dqkv_ref[:, v_cols] = tn(probs_b, front).astype(BF16)
        weighed = probs * dprobs
        dscore = probs * (dprobs - jnp.sum(weighed, axis=-1, keepdims=True))
        dscore_b = dscore.astype(BF16)
        dqkv_ref[:, cols] = (nn(dscore_b, key) * scale).astype(BF16)
        dqkv_ref[:, k_cols] = (tn(dscore_b, query) * scale).astype(BF16)


def attend(qkv, front, pairs):
    tokens, width = front.shape
    return pl.pallas_call(
        lambda *refs: attend_kernel(pairs, width, *refs),
        out_shape=(
            jax.ShapeDtypeStruct((tokens, width), BF16),
            jax.ShapeDtypeStruct((tokens, 3 * width), BF16),
        ),
        in_specs=[pl.BlockSpec(memory_space=pltpu.VMEM)] * 2,
        out_specs=(pl.BlockSpec(memory_space=pltpu.VMEM),) * 2,
        cost_estimate=pl.CostEstimate(
            flops=7 * 2 * tokens * tokens * width,
            bytes_accessed=16 * tokens * width,
            transcendentals=tokens * tokens * width // HS,
        ),
        name="attend",
    )(qkv, front)


FORWARD_A, FULL_A, FORWARD_B, FULL_B, LAST_A, LAST_B = 16, 24, 32, 40, 48, 51
COPIES = 54
RANK = {2: 0, 3: 1, 1: 2, 0: 3}


def reduce_kernel(n_ctx, rows, *refs):
    sources, ups, grads, atts = refs[0:4], refs[4:8], refs[8:12], refs[12:16]
    qkv_ref, proj_ref = refs[16:18]
    (x_all, u_all, d_all, t_all, own_a, own_b, got_a, got_b, fwd_a, fwd_b) = refs[18:28]
    full_a, full_b, last_a, last_b, load_sem, send_sem, recv_sem = refs[28:]
    tokens, width = atts[0].shape
    half = rows // 2
    dp, ctx, space = (lax.axis_index(name) for name in ("dp", "ctx", "space"))
    x, z, core = (ctx // 2 % 2) * 2 + dp, ctx // 4, ctx % 2

    def peer(dx, dz, dcore):
        px, pz, pc = (x + dx) % 4, (z + dz) % 4, (core + dcore) % 2
        return (px % 2, (pz * 2 + px // 2) * 2 + pc, space)

    loads = []
    for i, (group, into) in enumerate(
        ((sources, x_all), (ups, u_all), (grads, d_all), (atts, t_all))
    ):
        for u in range(4):
            loads.append(
                pltpu.make_async_copy(
                    group[u], into.at[pl.ds(u * tokens, tokens)], load_sem.at[i * 4 + u]
                )
            )
            loads[-1].start()

    barrier = pltpu.get_barrier_semaphore()
    near = [(0, 0, 1)] + [(d, 0, 0) for d in (1, 2, 3)] + [(0, d, 0) for d in (1, 2, 3)]
    for move in near:
        pl.semaphore_signal(
            barrier, inc=1, device_id=peer(*move), device_id_type=pl.DeviceIdType.MESH
        )
    pl.semaphore_wait(barrier, len(near))
    for load in loads:
        load.wait()

    def copy(source, target, at, to):
        return pltpu.make_async_remote_copy(
            src_ref=source,
            dst_ref=target,
            send_sem=send_sem.at[at],
            recv_sem=recv_sem.at[at],
            device_id=to,
            device_id_type=pl.DeviceIdType.MESH,
        )

    def far(t):
        k = t // 2
        return t % 2, (2 + k + (k // 2) * (1 + 2 * (k % 2))) % 4

    def swaps(t):
        return (
            copy(own_a.at[t, 1], got_a.at[t], 2 * t, peer(0, 0, 1)),
            copy(own_b.at[t, 1], got_b.at[t], 2 * t + 1, peer(0, 0, 1)),
        )

    def forward_a(t, dz, way):
        piece = own_a.at[t, 0, 1, pl.ds(way * half, half)]
        return copy(piece, fwd_a.at[way, dz], FORWARD_A + 2 * dz + way, peer(1 + 2 * way, 0, 0))

    def full_of_a(t, dz, way):
        return copy(own_a.at[t, 0, way], full_a.at[way, dz], FULL_A + 2 * dz + way, peer(1 + 2 * way, 0, 0))

    def forward_b(t, dx, hi, way):
        piece = own_b.at[t, 0, hi, pl.ds(way * half, half)]
        return copy(piece, fwd_b.at[way, dx], FORWARD_B + 2 * dx + way, peer(0, 1 + 2 * way, 0))

    def full_of_b(t, dx, hi, way):
        return copy(own_b.at[t, 0, hi], full_b.at[way, dx], FULL_B + 2 * dx + way, peer(0, 1 + 2 * way, 0))

    def compute(t):
        p, dz = far(t)
        off = pl.multiple_of(4 * rows * (((dp + p) % 2) * 4 + (z + dz) % 4), 128)
        start = ((x + p) % 4) // 2
        source = x_all[:, pl.ds(off, 4 * rows)]
        up = u_all[:, pl.ds(off, 4 * rows)]

        def put(ref, low, total):
            for hi in range(2):
                for c in range(2):
                    at = (2 * hi + c) * rows
                    ref[t, (c + 2 - core) % 2, (hi + 2 - start) % 2, :, low : low + total.shape[1]] = (
                        total[at : at + rows]
                    )

        put(own_a, 0, tn(source, d_all[:, : 2 * width]))
        put(own_b, 0, tn(source, d_all[:, 2 * width :]))
        put(own_b, width, tn(up, t_all[...]))
        for swap in swaps(t):
            swap.start()

    def pair_up(t):
        p, dz = far(t)
        for swap in swaps(t):
            swap.wait_recv()
        own_a[t, 0] += got_a[t]
        own_b[t, 0] += got_b[t]

        @pl.when(p == 0)
        def _():
            for way in range(2):
                forward_a(t, dz, way).start()

        @pl.when(dz == 2)
        def _():
            for hi in range(2):
                for way in range(2):
                    forward_b(t, p + 2 * hi, hi, way).start()

    def pass_on(t):
        p, dz = far(t)

        @pl.when(p == 1)
        def _():
            for way in range(2):
                forward_a(t, dz, way).wait_recv()
                own_a[t, 0, way, pl.ds(way * half, half)] += fwd_a[way, dz]
                full_of_a(t, dz, way).start()

        @pl.when(dz % 2 == 1)
        def _():
            way = dz // 2
            for hi in range(2):
                dx = p + 2 * hi
                forward_b(t, dx, hi, way).wait_recv()
                part = pl.ds(pl.multiple_of(way * half, half), half)
                own_b[t, 0, hi, part] += fwd_b[way, dx]
                full_of_b(t, dx, hi, way).start()

    def step(t, carry):
        @pl.when(t < 8)
        def _():
            compute(t)

        @pl.when((t >= 1) & (t < 9))
        def _():
            pair_up(t - 1)

        @pl.when(t >= 2)
        def _():
            pass_on(t - 2)

        return carry

    lax.fori_loop(0, 10, step, 0)

    def finish_a(dz):
        t = 2 * RANK[dz]
        for way in range(2):
            full_of_a(t, dz, way).wait_recv()
        own_a[t, 0, 0] += full_a[0, dz] + full_a[1, dz]

    def finish_b(dx):
        t, hi = 6 + dx % 2, dx // 2
        for way in range(2):
            full_of_b(t, dx, hi, way).wait_recv()
        own_b[t, 0, hi] += full_b[0, dx] + full_b[1, dx]

    def last_of_a(dz):
        return copy(own_a.at[2 * RANK[dz], 0, 0], last_a.at[dz - 1], LAST_A + dz - 1, peer(0, dz, 0))

    def last_of_b(dx):
        return copy(own_b.at[6 + dx % 2, 0, dx // 2], last_b.at[dx - 1], LAST_B + dx - 1, peer(dx, 0, 0))

    for d in (2, 3, 1):
        finish_a(d)
        last_of_a(d).start()
        finish_b(d)
        last_of_b(d).start()
    finish_a(0)
    finish_b(0)
    for d in (2, 3, 1):
        last_of_a(d).wait_recv()
        last_of_b(d).wait_recv()
    sum_a = own_a[6, 0, 0] + last_a[0] + last_a[1] + last_a[2]
    sum_b = own_b[6, 0, 0] + last_b[0] + last_b[1] + last_b[2]
    qkv_ref[0] = sum_a[:, :width]
    qkv_ref[1] = sum_a[:, width:]
    qkv_ref[2] = sum_b[:, :width]
    proj_ref[...] = sum_b[:, width:]

    def drain(t, carry):
        p, dz = far(t)
        for swap in swaps(t):
            swap.wait_send()

        @pl.when(p == 0)
        def _():
            for way in range(2):
                forward_a(t, dz, way).wait_send()

        @pl.when(p == 1)
        def _():
            for way in range(2):
                full_of_a(t, dz, way).wait_send()

        @pl.when(dz == 2)
        def _():
            for hi in range(2):
                for way in range(2):
                    forward_b(t, p + 2 * hi, hi, way).wait_send()

        @pl.when(dz % 2 == 1)
        def _():
            for hi in range(2):
                full_of_b(t, p + 2 * hi, hi, dz // 2).wait_send()

        return carry

    lax.fori_loop(0, 8, drain, 0)
    for d in (2, 3, 1):
        last_of_a(d).wait_send()
        last_of_b(d).wait_send()


def reduced_grads(n_ctx, rows, sources, ups, grads, atts):
    tokens, model = sources[0].shape
    width = atts[0].shape[1]
    wide = 2 * width
    vmem = pltpu.VMEM
    return pl.pallas_call(
        lambda *refs: reduce_kernel(n_ctx, rows, *refs),
        out_shape=(
            jax.ShapeDtypeStruct((3, rows, width), F32),
            jax.ShapeDtypeStruct((rows, width), F32),
        ),
        in_specs=[pl.BlockSpec(memory_space=pl.ANY)] * 16,
        out_specs=(pl.BlockSpec(memory_space=vmem),) * 2,
        scratch_shapes=[
            vmem((4 * tokens, model), BF16),
            vmem((4 * tokens, model), BF16),
            vmem((4 * tokens, 3 * width), BF16),
            vmem((4 * tokens, width), BF16),
            vmem((8, 2, 2, rows, wide), F32),
            vmem((8, 2, 2, rows, wide), F32),
            vmem((8, 2, rows, wide), F32),
            vmem((8, 2, rows, wide), F32),
            vmem((2, 4, rows // 2, wide), F32),
            vmem((2, 4, rows // 2, wide), F32),
            vmem((2, 4, rows, wide), F32),
            vmem((2, 4, rows, wide), F32),
            vmem((3, rows, wide), F32),
            vmem((3, rows, wide), F32),
            pltpu.SemaphoreType.DMA((16,)),
            pltpu.SemaphoreType.DMA((COPIES,)),
            pltpu.SemaphoreType.DMA((COPIES,)),
        ],
        compiler_params=pltpu.CompilerParams(
            collective_id=0, has_side_effects=True, vmem_limit_bytes=67043328
        ),
        cost_estimate=pl.CostEstimate(
            flops=2 * 4 * tokens * model * 4 * width,
            bytes_accessed=300 * 1024 * 1024,
            transcendentals=0,
        ),
        name="reduce",
    )(*sources, *ups, *grads, *atts)


def solution(mesh):
    n_dp, n_ctx, n_space = mesh.shape["dp"], mesh.shape["ctx"], mesh.shape["space"]

    def space_shift(array, by):
        return lax.ppermute(
            array, "space", [(i, (i + by) % n_space) for i in range(n_space)]
        )

    def body(inputs, upstream, qkv_weight, out_weight):
        clips, single, patches, model = inputs.shape
        width = out_weight.shape[1]
        pairs = clips * patches // n_ctx
        tokens = n_ctx * pairs
        weight = jnp.transpose(qkv_weight, (1, 0, 2)).reshape(model, 3 * width)

        def to_frames(array):
            array = array.reshape(n_ctx, pairs, model)
            array = lax.all_to_all(array, "ctx", 0, 0, tiled=True)
            return array.reshape(tokens, model)

        def gather(own):
            behind, ahead = space_shift(own, 1), space_shift(own, -1)
            half = tokens // 2
            across = jnp.concatenate(
                [space_shift(behind[:half], 1), space_shift(ahead[half:], -1)]
            )
            return [own, behind, ahead, across]

        sources = gather(to_frames(inputs))
        up_sources = gather(to_frames(upstream))
        attended, gradients, parts = [], [], []
        for source, up_source in zip(sources, up_sources):
            qkv = nn(source, weight).astype(BF16)
            front = nn(up_source, out_weight).astype(BF16)
            att, dqkv = attend(qkv, front, pairs)
            attended.append(att)
            gradients.append(dqkv)
            parts.append(nt(dqkv, weight).astype(BF16))

        gradients[3], parts = lax.optimization_barrier((gradients[3], parts))
        rows = model // (n_dp * n_ctx)
        qkv_grad, proj_grad = reduced_grads(
            n_ctx, rows, sources, up_sources, gradients, attended
        )

        back = [
            parts[0],
            space_shift(parts[1], -1),
            space_shift(parts[2], 1),
            space_shift(parts[3], 2),
        ]
        back, qkv_grad = lax.optimization_barrier((back, qkv_grad))
        total = sum(part.astype(F32) for part in back).astype(BF16)
        total = lax.all_to_all(total.reshape(n_ctx, pairs, model), "ctx", 0, 0, tiled=True)
        return total.reshape(clips, single, patches, model), qkv_grad, proj_grad

    placed = (
        P("dp", "ctx", "space", None),
        P("dp", "ctx", "space", None),
        P(None, None, "space"),
        P(None, "space"),
    )
    return jax.shard_map(
        body,
        mesh=mesh,
        in_specs=placed,
        out_specs=(
            P("dp", "ctx", "space", None),
            P(None, ("dp", "ctx"), "space"),
            P(("dp", "ctx"), "space"),
        ),
        check_vma=False,
    )
```

```python
import math

import jax
import jax.numpy as jnp
from jax import lax
from jax.experimental import pallas as pl
from jax.experimental.pallas import tpu as pltpu
from jax.sharding import PartitionSpec as P


HS = 128
F32 = jnp.float32
BF16 = jnp.bfloat16


def nn(a, b):
    return lax.dot_general(a, b, (((1,), (0,)), ((), ())), preferred_element_type=F32)


def nt(a, b):
    return lax.dot_general(a, b, (((1,), (1,)), ((), ())), preferred_element_type=F32)


def tn(a, b):
    return lax.dot_general(a, b, (((0,), (0,)), ((), ())), preferred_element_type=F32)


def attend_heads(pairs, unit, qkv_ref, front_ref, att_ref, dqkv_ref):
    tokens, width = front_ref.shape
    scale = 1.0 / math.sqrt(HS)
    row = lax.broadcasted_iota(jnp.int32, (tokens, tokens), 0)
    col = lax.broadcasted_iota(jnp.int32, (tokens, tokens), 1)
    valid = (row >= col) & (row % pairs == col % pairs)
    for head in range(width // HS):
        cols = slice(head * HS, (head + 1) * HS)
        k_cols = slice(width + head * HS, width + (head + 1) * HS)
        v_cols = slice(2 * width + head * HS, 2 * width + (head + 1) * HS)
        query, key, value = (qkv_ref[unit, s, :, cols] for s in range(3))
        front = front_ref[:, cols]
        masked = jnp.where(valid, nt(query, key) * scale, F32(-1e30))
        top = jnp.max(masked, axis=-1, keepdims=True)
        expo = jnp.where(valid, jnp.exp(masked - top), F32(0.0))
        probs = expo / jnp.sum(expo, axis=-1, keepdims=True)
        probs_b = probs.astype(BF16)
        att_ref[unit, :, cols] = nn(probs_b, value).astype(BF16)
        dprobs = nt(front, value)
        dqkv_ref[unit, :, v_cols] = tn(probs_b, front).astype(BF16)
        weighed = probs * dprobs
        dscore = probs * (dprobs - jnp.sum(weighed, axis=-1, keepdims=True))
        dscore_b = dscore.astype(BF16)
        dqkv_ref[unit, :, cols] = (nn(dscore_b, key) * scale).astype(BF16)
        dqkv_ref[unit, :, k_cols] = (tn(dscore_b, query) * scale).astype(BF16)


def enter_kernel(n_ctx, n_space, *refs):
    given, (weight_ref, out_weight_ref) = refs[0:2], refs[2:4]
    x_out, u_out, d_out, t_out = refs[4:8]
    part_out = refs[8:12]
    x_all, u_all, w_all, qkv_all, front, d_all, t_all, part_all = refs[12:20]
    load_sem, store_sem, swap_send, swap_recv, ring_send, ring_recv = refs[20:]
    every = (x_all, u_all)
    tokens, model = given[0].shape
    width = out_weight_ref.shape[1]
    pairs = tokens // n_ctx
    half = tokens // 2
    dp, ctx, space = (lax.axis_index(name) for name in ("dp", "ctx", "space"))

    loads = [
        pltpu.make_async_copy(weight_ref, w_all.at[pl.ds(0, 3)], load_sem.at[0]),
        pltpu.make_async_copy(out_weight_ref, w_all.at[3], load_sem.at[1]),
    ]
    for a in range(2):
        mine = pl.ds(pl.multiple_of(ctx * pairs, pairs), pairs)
        loads.append(
            pltpu.make_async_copy(given[a].at[mine], every[a].at[0, mine], load_sem.at[2 + a])
        )
    for load in loads:
        load.start()

    def signal(to):
        pl.semaphore_signal(
            pltpu.get_barrier_semaphore(), inc=1, device_id=to, device_id_type=pl.DeviceIdType.MESH
        )

    def greet(r, carry):
        signal((dp, (ctx + r) % n_ctx, space))
        return carry

    lax.fori_loop(1, n_ctx, greet, 0)
    for way in range(2):
        signal((dp, ctx, (space + 1 + 2 * way) % n_space))
    pl.semaphore_wait(pltpu.get_barrier_semaphore(), n_ctx + 1)

    def copy(source, target, send, recv, to):
        return pltpu.make_async_remote_copy(
            src_ref=source,
            dst_ref=target,
            send_sem=send,
            recv_sem=recv,
            device_id=to,
            device_id_type=pl.DeviceIdType.MESH,
        )

    def rows_of(member):
        return pl.ds(pl.multiple_of(member * pairs, pairs), pairs)

    def swap(a, r):
        to = (ctx + r) % n_ctx
        return copy(
            given[a].at[rows_of(to)],
            every[a].at[0, rows_of(ctx)],
            swap_send.at[a, r],
            swap_recv.at[a, r],
            (dp, to, space),
        )

    def arrival(a, r):
        frm = (ctx + n_ctx - r) % n_ctx
        return copy(
            given[a].at[rows_of(frm)],
            every[a].at[0, rows_of(frm)],
            swap_send.at[a, r],
            swap_recv.at[a, r],
            (dp, frm, space),
        )

    def near(a, h, way):
        part = pl.ds(h * half, half)
        at = a * 6 + h * 2 + way
        return copy(
            every[a].at[0, part],
            every[a].at[1 + way, part],
            ring_send.at[at],
            ring_recv.at[at],
            (dp, ctx, (space + 1 + 2 * way) % n_space),
        )

    def onward(a, way):
        part = pl.ds(way * half, half)
        at = a * 6 + 4 + way
        return copy(
            every[a].at[1 + way, part],
            every[a].at[3, part],
            ring_send.at[at],
            ring_recv.at[at],
            (dp, ctx, (space + 1 + 2 * way) % n_space),
        )

    for a in range(2):

        def begin(r, carry, a=a):
            swap(a, r).start()
            return carry

        lax.fori_loop(1, n_ctx, begin, 0)

    def spread(a):
        loads[2 + a].wait()
        for h in range(2):

            def settle(frame, carry, a=a):
                r = (ctx + n_ctx - frame) % n_ctx

                @pl.when(r > 0)
                def _():
                    arrival(a, r).wait_recv()

                return carry

            lax.fori_loop(h * n_ctx // 2, (h + 1) * n_ctx // 2, settle, 0)
            for way in range(2):
                near(a, h, way).start()

    def receive(a):
        for way in range(2):
            near(a, way, way).wait_recv()
            onward(a, way).start()
        for way in range(2):
            near(a, 1 - way, way).wait_recv()

    def stores(unit):
        return (
            pltpu.make_async_copy(x_all.at[unit], x_out.at[unit], store_sem.at[0, unit]),
            pltpu.make_async_copy(u_all.at[unit], u_out.at[unit], store_sem.at[1, unit]),
            pltpu.make_async_copy(d_all.at[unit], d_out.at[unit], store_sem.at[2, unit]),
            pltpu.make_async_copy(t_all.at[unit], t_out.at[unit], store_sem.at[3, unit]),
        )

    def part_store(unit):
        return pltpu.make_async_copy(part_all.at[unit], part_out[unit], store_sem.at[4, unit])

    def project(unit):
        def one(s, carry):
            qkv_all[unit, s] = nn(x_all[unit], w_all[s]).astype(BF16)
            return carry

        lax.fori_loop(0, 3, one, 0)

    def finish(unit):
        front[...] = nn(u_all[unit], w_all[3]).astype(BF16)
        attend_heads(pairs, unit, qkv_all, front, t_all, d_all)
        block = model // 6

        def columns(c, carry):
            at = pl.ds(pl.multiple_of(c * block, block), block)
            total = nt(d_all[unit, :, 0:width], w_all[0, at, :])
            total += nt(d_all[unit, :, width : 2 * width], w_all[1, at, :])
            total += nt(d_all[unit, :, 2 * width :], w_all[2, at, :])
            part_all[unit, :, at] = total.astype(BF16)
            return carry

        lax.fori_loop(0, 6, columns, 0)
        for store in stores(unit):
            store.start()
        for u in range(4):

            @pl.when(unit == u)
            def _(u=u):
                part_store(u).start()

    def step(s, carry):
        group = (s // 2 + 1) // 2
        unit = group + (group % 2) * (s % 2) + group // 2
        first = (s == 0) | (s == 2) | (s == 3) | (s == 6)

        @pl.when(s == 0)
        def _():
            spread(0)
            loads[0].wait()
            loads[1].wait()

        @pl.when(s == 1)
        def _():
            spread(1)

        @pl.when(s == 2)
        def _():
            receive(0)

        @pl.when(s == 4)
        def _():
            receive(1)

        @pl.when(s == 6)
        def _():
            for way in range(2):
                onward(0, way).wait_recv()

        @pl.when(s == 7)
        def _():
            for way in range(2):
                onward(1, way).wait_recv()

        @pl.when(first)
        def _():
            project(unit)

        @pl.when(jnp.logical_not(first))
        def _():
            finish(unit)

        return carry

    lax.fori_loop(0, 8, step, 0)

    for a in range(2):

        def drain(r, carry, a=a):
            swap(a, r).wait_send()
            return carry

        lax.fori_loop(1, n_ctx, drain, 0)
        for way in range(2):
            for h in range(2):
                near(a, h, way).wait_send()
            onward(a, way).wait_send()
    for u in range(4):
        for store in stores(u):
            store.wait()
        part_store(u).wait()


def enter(n_ctx, n_space, inputs, upstream, qkv_weight, out_weight):
    tokens, model = inputs.shape
    width = out_weight.shape[1]
    vmem = pltpu.VMEM

    def shape(*extent):
        return jax.ShapeDtypeStruct(extent, BF16)

    return pl.pallas_call(
        lambda *refs: enter_kernel(n_ctx, n_space, *refs),
        out_shape=(
            shape(4, tokens, model),
            shape(4, tokens, model),
            shape(4, tokens, 3 * width),
            shape(4, tokens, width),
        )
        + (shape(tokens, model),) * 4,
        in_specs=[pl.BlockSpec(memory_space=pl.ANY)] * 4,
        out_specs=(pl.BlockSpec(memory_space=pl.ANY),) * 8,
        scratch_shapes=[
            vmem((4, tokens, model), BF16),
            vmem((4, tokens, model), BF16),
            vmem((4, model, width), BF16),
            vmem((4, 3, tokens, width), BF16),
            vmem((tokens, width), BF16),
            vmem((4, tokens, 3 * width), BF16),
            vmem((4, tokens, width), BF16),
            vmem((4, tokens, model), BF16),
            pltpu.SemaphoreType.DMA((4,)),
            pltpu.SemaphoreType.DMA((5, 4)),
            pltpu.SemaphoreType.DMA((2, n_ctx)),
            pltpu.SemaphoreType.DMA((2, n_ctx)),
            pltpu.SemaphoreType.DMA((12,)),
            pltpu.SemaphoreType.DMA((12,)),
        ],
        compiler_params=pltpu.CompilerParams(
            collective_id=1, has_side_effects=True, vmem_limit_bytes=62000000
        ),
        name="enter",
    )(inputs, upstream, qkv_weight, out_weight)


FORWARD_A, FULL_A, FORWARD_B, FULL_B, LAST_A, LAST_B = 16, 24, 32, 40, 48, 51
COPIES = 54
RANK = {2: 0, 3: 1, 1: 2, 0: 3}


def reduce_kernel(n_ctx, rows, *refs):
    given = refs[0:4]
    qkv_ref, proj_ref = refs[4:6]
    (x_all, u_all, d_all, t_all, own_a, own_b, got_a, got_b, fwd_a, fwd_b) = refs[6:16]
    full_a, full_b, last_a, last_b, load_sem, send_sem, recv_sem = refs[16:]
    width = given[3].shape[1]
    half = rows // 2
    dp, ctx, space = (lax.axis_index(name) for name in ("dp", "ctx", "space"))
    x, z, core = (ctx // 2 % 2) * 2 + dp, ctx // 4, ctx % 2

    def peer(dx, dz, dcore):
        px, pz, pc = (x + dx) % 4, (z + dz) % 4, (core + dcore) % 2
        return (px % 2, (pz * 2 + px // 2) * 2 + pc, space)

    loads = [
        pltpu.make_async_copy(source, into, load_sem.at[i])
        for i, (source, into) in enumerate(zip(given, (x_all, u_all, d_all, t_all)))
    ]
    for load in loads:
        load.start()

    barrier = pltpu.get_barrier_semaphore()
    near = [(0, 0, 1)] + [(d, 0, 0) for d in (1, 2, 3)] + [(0, d, 0) for d in (1, 2, 3)]
    for move in near:
        pl.semaphore_signal(
            barrier, inc=1, device_id=peer(*move), device_id_type=pl.DeviceIdType.MESH
        )
    pl.semaphore_wait(barrier, len(near))
    for load in loads:
        load.wait()

    def copy(source, target, at, to):
        return pltpu.make_async_remote_copy(
            src_ref=source,
            dst_ref=target,
            send_sem=send_sem.at[at],
            recv_sem=recv_sem.at[at],
            device_id=to,
            device_id_type=pl.DeviceIdType.MESH,
        )

    def far(t):
        k = t // 2
        return t % 2, (2 + k + (k // 2) * (1 + 2 * (k % 2))) % 4

    def swaps(t):
        return (
            copy(own_a.at[t, 1], got_a.at[t], 2 * t, peer(0, 0, 1)),
            copy(own_b.at[t, 1], got_b.at[t], 2 * t + 1, peer(0, 0, 1)),
        )

    def forward_a(t, dz, way):
        piece = own_a.at[t, 0, 1, pl.ds(way * half, half)]
        return copy(piece, fwd_a.at[way, dz], FORWARD_A + 2 * dz + way, peer(1 + 2 * way, 0, 0))

    def full_of_a(t, dz, way):
        return copy(own_a.at[t, 0, way], full_a.at[way, dz], FULL_A + 2 * dz + way, peer(1 + 2 * way, 0, 0))

    def forward_b(t, dx, hi, way):
        piece = own_b.at[t, 0, hi, pl.ds(way * half, half)]
        return copy(piece, fwd_b.at[way, dx], FORWARD_B + 2 * dx + way, peer(0, 1 + 2 * way, 0))

    def full_of_b(t, dx, hi, way):
        return copy(own_b.at[t, 0, hi], full_b.at[way, dx], FULL_B + 2 * dx + way, peer(0, 1 + 2 * way, 0))

    def compute(t):
        p, dz = far(t)
        off = pl.multiple_of(4 * rows * (((dp + p) % 2) * 4 + (z + dz) % 4), 128)
        start = ((x + p) % 4) // 2
        source = x_all[:, pl.ds(off, 4 * rows)]
        up = u_all[:, pl.ds(off, 4 * rows)]

        def put(ref, low, total):
            for hi in range(2):
                for c in range(2):
                    at = (2 * hi + c) * rows
                    ref[t, (c + 2 - core) % 2, (hi + 2 - start) % 2, :, low : low + total.shape[1]] = (
                        total[at : at + rows]
                    )

        put(own_a, 0, tn(source, d_all[:, : 2 * width]))
        put(own_b, 0, tn(source, d_all[:, 2 * width :]))
        put(own_b, width, tn(up, t_all[...]))
        for swap in swaps(t):
            swap.start()

    def pair_up(t):
        p, dz = far(t)
        for swap in swaps(t):
            swap.wait_recv()
        own_a[t, 0] += got_a[t]
        own_b[t, 0] += got_b[t]

        @pl.when(p == 0)
        def _():
            for way in range(2):
                forward_a(t, dz, way).start()

        @pl.when(dz == 2)
        def _():
            for hi in range(2):
                for way in range(2):
                    forward_b(t, p + 2 * hi, hi, way).start()

    def pass_on(t):
        p, dz = far(t)

        @pl.when(p == 1)
        def _():
            for way in range(2):
                forward_a(t, dz, way).wait_recv()
                own_a[t, 0, way, pl.ds(way * half, half)] += fwd_a[way, dz]
                full_of_a(t, dz, way).start()

        @pl.when(dz % 2 == 1)
        def _():
            way = dz // 2
            for hi in range(2):
                dx = p + 2 * hi
                forward_b(t, dx, hi, way).wait_recv()
                part = pl.ds(pl.multiple_of(way * half, half), half)
                own_b[t, 0, hi, part] += fwd_b[way, dx]
                full_of_b(t, dx, hi, way).start()

    def step(t, carry):
        @pl.when(t < 8)
        def _():
            compute(t)

        @pl.when((t >= 1) & (t < 9))
        def _():
            pair_up(t - 1)

        @pl.when(t >= 2)
        def _():
            pass_on(t - 2)

        return carry

    lax.fori_loop(0, 10, step, 0)

    def finish_a(dz):
        t = 2 * RANK[dz]
        for way in range(2):
            full_of_a(t, dz, way).wait_recv()
        own_a[t, 0, 0] += full_a[0, dz] + full_a[1, dz]

    def finish_b(dx):
        t, hi = 6 + dx % 2, dx // 2
        for way in range(2):
            full_of_b(t, dx, hi, way).wait_recv()
        own_b[t, 0, hi] += full_b[0, dx] + full_b[1, dx]

    def last_of_a(dz):
        return copy(own_a.at[2 * RANK[dz], 0, 0], last_a.at[dz - 1], LAST_A + dz - 1, peer(0, dz, 0))

    def last_of_b(dx):
        return copy(own_b.at[6 + dx % 2, 0, dx // 2], last_b.at[dx - 1], LAST_B + dx - 1, peer(dx, 0, 0))

    for d in (2, 3, 1):
        finish_a(d)
        last_of_a(d).start()
        finish_b(d)
        last_of_b(d).start()
    finish_a(0)
    finish_b(0)
    for d in (2, 3, 1):
        last_of_a(d).wait_recv()
        last_of_b(d).wait_recv()
    sum_a = own_a[6, 0, 0] + last_a[0] + last_a[1] + last_a[2]
    sum_b = own_b[6, 0, 0] + last_b[0] + last_b[1] + last_b[2]
    qkv_ref[0] = sum_a[:, :width]
    qkv_ref[1] = sum_a[:, width:]
    qkv_ref[2] = sum_b[:, :width]
    proj_ref[...] = sum_b[:, width:]

    def drain(t, carry):
        p, dz = far(t)
        for swap in swaps(t):
            swap.wait_send()

        @pl.when(p == 0)
        def _():
            for way in range(2):
                forward_a(t, dz, way).wait_send()

        @pl.when(p == 1)
        def _():
            for way in range(2):
                full_of_a(t, dz, way).wait_send()

        @pl.when(dz == 2)
        def _():
            for hi in range(2):
                for way in range(2):
                    forward_b(t, p + 2 * hi, hi, way).wait_send()

        @pl.when(dz % 2 == 1)
        def _():
            for hi in range(2):
                full_of_b(t, p + 2 * hi, hi, dz // 2).wait_send()

        return carry

    lax.fori_loop(0, 8, drain, 0)
    for d in (2, 3, 1):
        last_of_a(d).wait_send()
        last_of_b(d).wait_send()


def reduced_grads(n_ctx, rows, sources, ups, grads, atts):
    tokens, model = sources.shape
    width = atts.shape[1]
    wide = 2 * width
    vmem = pltpu.VMEM
    return pl.pallas_call(
        lambda *refs: reduce_kernel(n_ctx, rows, *refs),
        out_shape=(
            jax.ShapeDtypeStruct((3, rows, width), F32),
            jax.ShapeDtypeStruct((rows, width), F32),
        ),
        in_specs=[pl.BlockSpec(memory_space=pl.ANY)] * 4,
        out_specs=(pl.BlockSpec(memory_space=vmem),) * 2,
        scratch_shapes=[
            vmem((tokens, model), BF16),
            vmem((tokens, model), BF16),
            vmem((tokens, 3 * width), BF16),
            vmem((tokens, width), BF16),
            vmem((8, 2, 2, rows, wide), F32),
            vmem((8, 2, 2, rows, wide), F32),
            vmem((8, 2, rows, wide), F32),
            vmem((8, 2, rows, wide), F32),
            vmem((2, 4, rows // 2, wide), F32),
            vmem((2, 4, rows // 2, wide), F32),
            vmem((2, 4, rows, wide), F32),
            vmem((2, 4, rows, wide), F32),
            vmem((3, rows, wide), F32),
            vmem((3, rows, wide), F32),
            pltpu.SemaphoreType.DMA((4,)),
            pltpu.SemaphoreType.DMA((COPIES,)),
            pltpu.SemaphoreType.DMA((COPIES,)),
        ],
        compiler_params=pltpu.CompilerParams(
            collective_id=0, has_side_effects=True, vmem_limit_bytes=67043328
        ),
        cost_estimate=pl.CostEstimate(
            flops=2 * tokens * model * 4 * width,
            bytes_accessed=300 * 1024 * 1024,
            transcendentals=0,
        ),
        name="reduce",
    )(sources, ups, grads, atts)


def solution(mesh):
    n_dp, n_ctx, n_space = mesh.shape["dp"], mesh.shape["ctx"], mesh.shape["space"]

    def space_shift(array, by):
        return lax.ppermute(
            array, "space", [(i, (i + by) % n_space) for i in range(n_space)]
        )

    def body(inputs, upstream, qkv_weight, out_weight):
        clips, single, patches, model = inputs.shape
        pairs = clips * patches // n_ctx
        tokens = n_ctx * pairs
        *work, part_own, part_behind, part_ahead, part_across = enter(
            n_ctx,
            n_space,
            inputs.reshape(tokens, model),
            upstream.reshape(tokens, model),
            qkv_weight,
            out_weight,
        )

        rows = model // (n_dp * n_ctx)
        qkv_grad, proj_grad = reduced_grads(
            n_ctx, rows, *(w.reshape(4 * tokens, w.shape[2]) for w in work)
        )

        back = [
            part_own,
            space_shift(part_behind, -1),
            space_shift(part_ahead, 1),
            space_shift(part_across, 2),
        ]
        back, qkv_grad = lax.optimization_barrier((back, qkv_grad))
        total = sum(part.astype(F32) for part in back).astype(BF16)
        total = lax.all_to_all(total.reshape(n_ctx, pairs, model), "ctx", 0, 0, tiled=True)
        return total.reshape(clips, single, patches, model), qkv_grad, proj_grad

    placed = (
        P("dp", "ctx", "space", None),
        P("dp", "ctx", "space", None),
        P(None, None, "space"),
        P(None, "space"),
    )
    return jax.shard_map(
        body,
        mesh=mesh,
        in_specs=placed,
        out_specs=(
            P("dp", "ctx", "space", None),
            P(None, ("dp", "ctx"), "space"),
            P(("dp", "ctx"), "space"),
        ),
        check_vma=False,
    )
```

```python
import math

import jax
import jax.numpy as jnp
from jax import lax
from jax.experimental import pallas as pl
from jax.experimental.pallas import tpu as pltpu
from jax.sharding import PartitionSpec as P

HS = 128
F32 = jnp.float32
BF16 = jnp.bfloat16


def nn(a, b):
    return lax.dot_general(a, b, (((1,), (0,)), ((), ())), preferred_element_type=F32)


def nt(a, b):
    return lax.dot_general(a, b, (((1,), (1,)), ((), ())), preferred_element_type=F32)


def tn(a, b):
    return lax.dot_general(a, b, (((0,), (0,)), ((), ())), preferred_element_type=F32)


def attend_heads(pairs, slot, mine, qkv_ref, front_ref, att_ref, dqkv_ref):
    tokens, width = front_ref.shape
    scale = 1.0 / math.sqrt(HS)
    row = lax.broadcasted_iota(jnp.int32, (tokens, tokens), 0)
    col = lax.broadcasted_iota(jnp.int32, (tokens, tokens), 1)
    valid = (row >= col) & (row % pairs == col % pairs)
    for head in range(width // HS):
        cols = slice(head * HS, (head + 1) * HS)
        k_cols = slice(width + head * HS, width + (head + 1) * HS)
        v_cols = slice(2 * width + head * HS, 2 * width + (head + 1) * HS)
        query, key, value = (qkv_ref[slot, s, :, cols] for s in range(3))
        front = front_ref[:, cols]
        masked = jnp.where(valid, nt(query, key) * scale, F32(-1e30))
        top = jnp.max(masked, axis=-1, keepdims=True)
        expo = jnp.where(valid, jnp.exp(masked - top), F32(0.0))
        probs = expo / jnp.sum(expo, axis=-1, keepdims=True)
        probs_b = probs.astype(BF16)
        att_ref[mine, cols] = nn(probs_b, value).astype(BF16)
        dprobs = nt(front, value)
        dqkv_ref[mine, v_cols] = tn(probs_b, front).astype(BF16)
        weighed = probs * dprobs
        dscore = probs * (dprobs - jnp.sum(weighed, axis=-1, keepdims=True))
        dscore_b = dscore.astype(BF16)
        dqkv_ref[mine, cols] = (nn(dscore_b, key) * scale).astype(BF16)
        dqkv_ref[mine, k_cols] = (tn(dscore_b, query) * scale).astype(BF16)


FORWARD_A, FULL_A, FORWARD_B, FULL_B, LAST_A, LAST_B = 16, 24, 32, 40, 48, 51
COPIES = 54
RANK = {2: 0, 3: 1, 1: 2, 0: 3}


def whole_kernel(n_ctx, n_space, rows, *refs):
    given, (weight_ref, out_weight_ref) = refs[0:2], refs[2:4]
    input_ref, qkv_ref, proj_ref = refs[4:7]
    x_all, u_all, w_all, qkv_two, front, d_all, t_all, part_all, landed = refs[7:16]
    keep_a, keep_b, send_a, send_b, got_a, got_b, fwd_a, fwd_b, full_a, full_b, last_a, last_b = refs[16:28]
    load_sem, swap_send, swap_recv, ring_send, ring_recv = refs[28:33]
    send_sem, recv_sem, back_send, back_recv, out_send, out_recv = refs[33:]
    every = (x_all, u_all)
    tokens, model = given[0].shape
    width = out_weight_ref.shape[1]
    pairs = tokens // n_ctx
    frames = n_ctx // 4
    halved = tokens // 2
    half = rows // 2
    dp, ctx, space = (lax.axis_index(name) for name in ("dp", "ctx", "space"))
    x, z, core = (ctx // 2 % 2) * 2 + dp, ctx // 4, ctx % 2

    def peer(dx, dz, dcore):
        px, pz, pc = (x + dx) % 4, (z + dz) % 4, (core + dcore) % 2
        return (px % 2, (pz * 2 + px // 2) * 2 + pc, space)

    def frame_rows(first, count=1):
        return pl.ds(pl.multiple_of(first * pairs, pairs), count * pairs)

    def unit_rows(unit):
        return pl.ds(pl.multiple_of(unit * tokens, tokens), tokens)

    loads = [
        pltpu.make_async_copy(weight_ref, w_all.at[pl.ds(0, 3)], load_sem.at[0]),
        pltpu.make_async_copy(out_weight_ref, w_all.at[3], load_sem.at[1]),
    ]
    for a in range(2):
        mine = frame_rows(ctx)
        loads.append(pltpu.make_async_copy(given[a].at[mine], every[a].at[mine], load_sem.at[2 + a]))
    for load in loads:
        load.start()

    def signal(to):
        pl.semaphore_signal(
            pltpu.get_barrier_semaphore(), inc=1, device_id=to, device_id_type=pl.DeviceIdType.MESH
        )

    def greet(r, carry):
        signal((dp, (ctx + r) % n_ctx, space))
        return carry

    lax.fori_loop(1, n_ctx, greet, 0)
    for d in range(1, n_space):
        signal((dp, ctx, (space + d) % n_space))
    for d in (1, 3):
        signal(peer(d, 0, 0))
    pl.semaphore_wait(pltpu.get_barrier_semaphore(), n_ctx - 1 + n_space - 1 + 2)

    def send(source, target, send_at, recv_at, to):
        return pltpu.make_async_remote_copy(
            src_ref=source,
            dst_ref=target,
            send_sem=send_at,
            recv_sem=recv_at,
            device_id=to,
            device_id_type=pl.DeviceIdType.MESH,
        )

    def swap(a, r):
        to = (ctx + r) % n_ctx
        return send(
            given[a].at[frame_rows(to)],
            every[a].at[frame_rows(ctx)],
            swap_send.at[a, r],
            swap_recv.at[a, r],
            (dp, to, space),
        )

    def arrival(a, r):
        frm = (ctx + n_ctx - r) % n_ctx
        return send(
            given[a].at[frame_rows(frm)],
            every[a].at[frame_rows(frm)],
            swap_send.at[a, r],
            swap_recv.at[a, r],
            (dp, frm, space),
        )

    def beside(way):
        return (dp, ctx, (space + 1 + 2 * way) % n_space)

    def near(a, h, way):
        at = a * 6 + h * 2 + way
        return send(
            every[a].at[pl.ds(h * halved, halved)],
            every[a].at[pl.ds((1 + way) * tokens + h * halved, halved)],
            ring_send.at[at],
            ring_recv.at[at],
            beside(way),
        )

    def onward(a, way):
        at = a * 6 + 4 + way
        return send(
            every[a].at[pl.ds((1 + way) * tokens + way * halved, halved)],
            every[a].at[pl.ds(3 * tokens + way * halved, halved)],
            ring_send.at[at],
            ring_recv.at[at],
            beside(way),
        )

    for a in range(2):

        def begin(r, carry, a=a):
            swap(a, r).start()
            return carry

        lax.fori_loop(1, n_ctx, begin, 0)

    def spread(a):
        loads[2 + a].wait()
        for h in range(2):

            def settle(frame, carry, a=a):
                r = (ctx + n_ctx - frame) % n_ctx

                @pl.when(r > 0)
                def _():
                    arrival(a, r).wait_recv()

                return carry

            lax.fori_loop(h * n_ctx // 2, (h + 1) * n_ctx // 2, settle, 0)
            for way in range(2):
                near(a, h, way).start()

    def receive(a):
        for way in range(2):
            near(a, way, way).wait_recv()
            onward(a, way).start()
        for way in range(2):
            near(a, 1 - way, way).wait_recv()

    def group(q):
        return (z + 1 + q) % 4 * frames

    def back(q, which):
        part = frame_rows(group(q), frames)
        return send(
            part_all.at[1 + which, part],
            landed.at[which, part],
            back_send.at[q, which],
            back_recv.at[q, which],
            (dp, ctx, (space + (3, 1, 2)[which]) % n_space),
        )

    def outward(frame):
        return send(
            part_all.at[0, frame_rows(frame)],
            input_ref.at[frame_rows(ctx)],
            out_send.at[frame],
            out_recv.at[ctx],
            (dp, frame, space),
        )

    def inward(frame):
        return send(
            part_all.at[0, frame_rows(frame)],
            input_ref.at[frame_rows(frame)],
            out_send.at[frame],
            out_recv.at[frame],
            (dp, frame, space),
        )

    def kept():
        at = frame_rows(ctx)
        return pltpu.make_async_copy(part_all.at[0, at], input_ref.at[at], load_sem.at[4])

    def quarter(q):
        for which in range(3):
            back(q, which).wait_recv()

        def one(i, carry):
            frame = group(q) + i
            at = frame_rows(frame)
            total = part_all[0, at].astype(F32)
            for which in range(3):
                total += landed[which, at].astype(F32)
            part_all[0, at] = total.astype(BF16)

            @pl.when(frame == ctx)
            def _():
                kept().start()

            @pl.when(frame != ctx)
            def _():
                outward(frame).start()

            return carry

        lax.fori_loop(0, frames, one, 0)

    def project(unit):
        def one(s, carry):
            qkv_two[unit % 2, s] = nn(x_all[unit_rows(unit)], w_all[s]).astype(BF16)
            return carry

        lax.fori_loop(0, 3, one, 0)

    def finish(unit):
        mine = unit_rows(unit)
        front[...] = nn(u_all[mine], w_all[3]).astype(BF16)
        attend_heads(pairs, unit % 2, mine, qkv_two, front, t_all, d_all)
        block = model // 6

        def columns(c, carry):
            at = pl.ds(pl.multiple_of(c * block, block), block)
            total = nt(d_all[mine, 0:width], w_all[0, at, :])
            total += nt(d_all[mine, width : 2 * width], w_all[1, at, :])
            total += nt(d_all[mine, 2 * width :], w_all[2, at, :])
            part_all[unit, :, at] = total.astype(BF16)
            return carry

        lax.fori_loop(0, 6, columns, 0)
        for which in range(3):

            @pl.when(unit == 1 + which)
            def _(which=which):
                for q in range(4):
                    back(q, which).start()

    def step(s, carry):
        pace = (s // 2 + 1) // 2
        unit = pace + (pace % 2) * (s % 2) + pace // 2
        first = (s == 0) | (s == 2) | (s == 3) | (s == 6)

        @pl.when(s == 0)
        def _():
            spread(0)
            loads[0].wait()
            loads[1].wait()

        @pl.when(s == 1)
        def _():
            spread(1)

        @pl.when(s == 2)
        def _():
            receive(0)

        @pl.when(s == 4)
        def _():
            receive(1)

        @pl.when(s == 6)
        def _():
            for way in range(2):
                onward(0, way).wait_recv()

        @pl.when(s == 7)
        def _():
            for way in range(2):
                onward(1, way).wait_recv()

        @pl.when(first)
        def _():
            project(unit)

        @pl.when(jnp.logical_not(first))
        def _():
            finish(unit)

        return carry

    lax.fori_loop(0, 8, step, 0)

    def copy(source, target, at, to):
        return send(source, target, send_sem.at[at], recv_sem.at[at], to)

    def far(t):
        k = t // 2
        return t % 2, (2 + k + (k // 2) * (1 + 2 * (k % 2))) % 4

    def trades(t):
        return (
            copy(send_a.at[t % 2], got_a.at[t % 4], 2 * t, peer(0, 0, 1)),
            copy(send_b.at[t % 2], got_b.at[t % 4], 2 * t + 1, peer(0, 0, 1)),
        )

    def forward_a(t, dz, way):
        piece = keep_a.at[t, 1, pl.ds(way * half, half)]
        return copy(piece, fwd_a.at[way, dz], FORWARD_A + 2 * dz + way, peer(1 + 2 * way, 0, 0))

    def full_of_a(t, dz, way):
        return copy(keep_a.at[t, way], full_a.at[way, dz], FULL_A + 2 * dz + way, peer(1 + 2 * way, 0, 0))

    def forward_b(t, dx, hi, way):
        piece = keep_b.at[t, hi, pl.ds(way * half, half)]
        return copy(piece, fwd_b.at[way, dx], FORWARD_B + 2 * dx + way, peer(0, 1 + 2 * way, 0))

    def full_of_b(t, dx, hi, way):
        return copy(keep_b.at[t, hi], full_b.at[way, dx], FULL_B + 2 * dx + way, peer(0, 1 + 2 * way, 0))

    def compute(t):
        p, dz = far(t)
        start = ((x + p) % 4) // 2
        off = 4 * rows * (((dp + p) % 2) * 4 + (z + dz) % 4)
        columns = pl.ds(pl.multiple_of(off, 128), 4 * rows)

        @pl.when(t >= 2)
        def _():
            for trade in trades(t - 2):
                trade.wait_send()

        def put(send_ref, keep_ref, low, total):
            high = low + total.shape[1]
            for hi in range(2):
                spot = (hi + 2 - start) % 2
                even = total[2 * hi * rows : (2 * hi + 1) * rows]
                odd = total[(2 * hi + 1) * rows : (2 * hi + 2) * rows]

                @pl.when(core == 0)
                def _():
                    keep_ref[t, spot, :, low:high] = even
                    send_ref[t % 2, spot, :, low:high] = odd

                @pl.when(core == 1)
                def _():
                    keep_ref[t, spot, :, low:high] = odd
                    send_ref[t % 2, spot, :, low:high] = even

        source = x_all[:, columns]
        put(send_a, keep_a, 0, tn(source, d_all[:, : 2 * width]))
        put(send_b, keep_b, 0, tn(source, d_all[:, 2 * width :]))
        put(send_b, keep_b, width, tn(u_all[:, columns], t_all[...]))
        for trade in trades(t):
            trade.start()

    def pair_up(t):
        p, dz = far(t)
        for trade in trades(t):
            trade.wait_recv()
        keep_a[t] += got_a[t % 4]
        keep_b[t] += got_b[t % 4]

        @pl.when(p == 0)
        def _():
            for way in range(2):
                forward_a(t, dz, way).start()

        @pl.when(dz == 2)
        def _():
            for hi in range(2):
                for way in range(2):
                    forward_b(t, p + 2 * hi, hi, way).start()

    def pass_on(t):
        p, dz = far(t)

        @pl.when(p == 1)
        def _():
            for way in range(2):
                forward_a(t, dz, way).wait_recv()
                keep_a[t, way, pl.ds(way * half, half)] += fwd_a[way, dz]
                full_of_a(t, dz, way).start()

        @pl.when(dz % 2 == 1)
        def _():
            way = dz // 2
            for hi in range(2):
                dx = p + 2 * hi
                forward_b(t, dx, hi, way).wait_recv()
                part = pl.ds(pl.multiple_of(way * half, half), half)
                keep_b[t, hi, part] += fwd_b[way, dx]
                full_of_b(t, dx, hi, way).start()

    def work(t, carry):
        @pl.when(t < 8)
        def _():
            compute(t)

        @pl.when((t >= 1) & (t < 9))
        def _():
            pair_up(t - 1)

        @pl.when(t >= 2)
        def _():
            pass_on(t - 2)

        return carry

    lax.fori_loop(0, 10, work, 0)

    def finish_a(dz):
        t = 2 * RANK[dz]
        for way in range(2):
            full_of_a(t, dz, way).wait_recv()
        keep_a[t, 0] += full_a[0, dz] + full_a[1, dz]

    def finish_b(dx):
        t, hi = 6 + dx % 2, dx // 2
        for way in range(2):
            full_of_b(t, dx, hi, way).wait_recv()
        keep_b[t, hi] += full_b[0, dx] + full_b[1, dx]

    def last_of_a(dz):
        return copy(keep_a.at[2 * RANK[dz], 0], last_a.at[dz - 1], LAST_A + dz - 1, peer(0, dz, 0))

    def last_of_b(dx):
        return copy(keep_b.at[6 + dx % 2, dx // 2], last_b.at[dx - 1], LAST_B + dx - 1, peer(dx, 0, 0))

    quarter(0)
    quarter(1)
    for d in (2, 3, 1):
        finish_a(d)
        last_of_a(d).start()
        finish_b(d)
        last_of_b(d).start()
    finish_a(0)
    finish_b(0)
    quarter(2)
    for d in (2, 3, 1):
        last_of_a(d).wait_recv()
        last_of_b(d).wait_recv()
    sum_a = keep_a[6, 0] + last_a[0] + last_a[1] + last_a[2]
    sum_b = keep_b[6, 0] + last_b[0] + last_b[1] + last_b[2]
    qkv_ref[0] = sum_a[:, :width]
    qkv_ref[1] = sum_a[:, width:]
    qkv_ref[2] = sum_b[:, :width]
    proj_ref[...] = sum_b[:, width:]
    quarter(3)

    def settle(frame, carry):
        @pl.when(frame == ctx)
        def _():
            kept().wait()

        @pl.when(frame != ctx)
        def _():
            outward(frame).wait_send()
            inward(frame).wait_recv()

        return carry

    lax.fori_loop(0, n_ctx, settle, 0)

    def home(q, carry):
        for which in range(3):
            back(q, which).wait_send()
        return carry

    lax.fori_loop(0, 4, home, 0)
    for a in range(2):

        def sent(r, carry, a=a):
            swap(a, r).wait_send()
            return carry

        lax.fori_loop(1, n_ctx, sent, 0)
        for way in range(2):
            for h in range(2):
                near(a, h, way).wait_send()
            onward(a, way).wait_send()
    for t in (6, 7):
        for trade in trades(t):
            trade.wait_send()

    def drain(t, carry):
        p, dz = far(t)

        @pl.when(p == 0)
        def _():
            for way in range(2):
                forward_a(t, dz, way).wait_send()

        @pl.when(p == 1)
        def _():
            for way in range(2):
                full_of_a(t, dz, way).wait_send()

        @pl.when(dz == 2)
        def _():
            for hi in range(2):
                for way in range(2):
                    forward_b(t, p + 2 * hi, hi, way).wait_send()

        @pl.when(dz % 2 == 1)
        def _():
            for hi in range(2):
                full_of_b(t, p + 2 * hi, hi, dz // 2).wait_send()

        return carry

    lax.fori_loop(0, 8, drain, 0)
    for d in (2, 3, 1):
        last_of_a(d).wait_send()
        last_of_b(d).wait_send()


def whole(n_ctx, n_space, rows, inputs, upstream, qkv_weight, out_weight):
    tokens, model = inputs.shape
    width = out_weight.shape[1]
    wide = 2 * width
    vmem, dma = pltpu.VMEM, pltpu.SemaphoreType.DMA
    return pl.pallas_call(
        lambda *refs: whole_kernel(n_ctx, n_space, rows, *refs),
        out_shape=(
            jax.ShapeDtypeStruct((tokens, model), BF16),
            jax.ShapeDtypeStruct((3, rows, width), F32),
            jax.ShapeDtypeStruct((rows, width), F32),
        ),
        in_specs=[pl.BlockSpec(memory_space=pl.ANY)] * 4,
        out_specs=(pl.BlockSpec(memory_space=pl.ANY),) + (pl.BlockSpec(memory_space=vmem),) * 2,
        scratch_shapes=[
            vmem((4 * tokens, model), BF16),
            vmem((4 * tokens, model), BF16),
            vmem((4, model, width), BF16),
            vmem((2, 3, tokens, width), BF16),
            vmem((tokens, width), BF16),
            vmem((4 * tokens, 3 * width), BF16),
            vmem((4 * tokens, width), BF16),
            vmem((4, tokens, model), BF16),
            vmem((3, tokens, model), BF16),
            vmem((8, 2, rows, wide), F32),
            vmem((8, 2, rows, wide), F32),
            vmem((2, 2, rows, wide), F32),
            vmem((2, 2, rows, wide), F32),
            vmem((4, 2, rows, wide), F32),
            vmem((4, 2, rows, wide), F32),
            vmem((2, 4, rows // 2, wide), F32),
            vmem((2, 4, rows // 2, wide), F32),
            vmem((2, 4, rows, wide), F32),
            vmem((2, 4, rows, wide), F32),
            vmem((3, rows, wide), F32),
            vmem((3, rows, wide), F32),
            dma((5,)),
            dma((2, n_ctx)),
            dma((2, n_ctx)),
            dma((12,)),
            dma((12,)),
            dma((COPIES,)),
            dma((COPIES,)),
            dma((4, 3)),
            dma((4, 3)),
            dma((n_ctx,)),
            dma((n_ctx,)),
        ],
        compiler_params=pltpu.CompilerParams(
            collective_id=0, has_side_effects=True, vmem_limit_bytes=67043328
        ),
        name="whole",
    )(inputs, upstream, qkv_weight, out_weight)


def solution(mesh):
    n_dp, n_ctx, n_space = mesh.shape["dp"], mesh.shape["ctx"], mesh.shape["space"]

    def body(inputs, upstream, qkv_weight, out_weight):
        clips, single, patches, model = inputs.shape
        tokens = clips * patches
        input_grad, qkv_grad, proj_grad = whole(
            n_ctx,
            n_space,
            model // (n_dp * n_ctx),
            inputs.reshape(tokens, model),
            upstream.reshape(tokens, model),
            qkv_weight,
            out_weight,
        )
        return input_grad.reshape(clips, single, patches, model), qkv_grad, proj_grad

    placed = (
        P("dp", "ctx", "space", None),
        P("dp", "ctx", "space", None),
        P(None, None, "space"),
        P(None, "space"),
    )
    return jax.shard_map(
        body,
        mesh=mesh,
        in_specs=placed,
        out_specs=(
            P("dp", "ctx", "space", None),
            P(None, ("dp", "ctx"), "space"),
            P(("dp", "ctx"), "space"),
        ),
        check_vma=False,
    )
```

```python
import math

import jax
import jax.numpy as jnp
from jax import lax
from jax.experimental import pallas as pl
from jax.experimental.pallas import tpu as pltpu
from jax.sharding import PartitionSpec as P

HS = 128
F32 = jnp.float32
BF16 = jnp.bfloat16


def nn(a, b):
    return lax.dot_general(a, b, (((1,), (0,)), ((), ())), preferred_element_type=F32)


def nt(a, b):
    return lax.dot_general(a, b, (((1,), (1,)), ((), ())), preferred_element_type=F32)


def tn(a, b):
    return lax.dot_general(a, b, (((0,), (0,)), ((), ())), preferred_element_type=F32)


def attend_heads(pairs, slot, mine, qkv_ref, front_ref, att_ref, dqkv_ref):
    tokens, width = front_ref.shape
    scale = 1.0 / math.sqrt(HS)
    row = lax.broadcasted_iota(jnp.int32, (tokens, tokens), 0)
    col = lax.broadcasted_iota(jnp.int32, (tokens, tokens), 1)
    valid = (row >= col) & (row % pairs == col % pairs)
    for head in range(width // HS):
        cols = slice(head * HS, (head + 1) * HS)
        k_cols = slice(width + head * HS, width + (head + 1) * HS)
        v_cols = slice(2 * width + head * HS, 2 * width + (head + 1) * HS)
        query, key, value = (qkv_ref[slot, s, :, cols] for s in range(3))
        front = front_ref[:, cols]
        masked = jnp.where(valid, nt(query, key) * scale, F32(-1e30))
        top = jnp.max(masked, axis=-1, keepdims=True)
        expo = jnp.where(valid, jnp.exp(masked - top), F32(0.0))
        probs = expo / jnp.sum(expo, axis=-1, keepdims=True)
        probs_b = probs.astype(BF16)
        att_ref[mine, cols] = nn(probs_b, value).astype(BF16)
        dprobs = nt(front, value)
        dqkv_ref[mine, v_cols] = tn(probs_b, front).astype(BF16)
        weighed = probs * dprobs
        dscore = probs * (dprobs - jnp.sum(weighed, axis=-1, keepdims=True))
        dscore_b = dscore.astype(BF16)
        dqkv_ref[mine, cols] = (nn(dscore_b, key) * scale).astype(BF16)
        dqkv_ref[mine, k_cols] = (tn(dscore_b, query) * scale).astype(BF16)


FORWARD_A, FULL_A, FORWARD_B, FULL_B, LAST_A, LAST_B = 16, 24, 32, 40, 48, 51
COPIES = 54
RANK = {2: 0, 3: 1, 1: 2, 0: 3}


def whole_kernel(n_ctx, n_space, rows, *refs):
    given, (weight_ref, out_weight_ref) = refs[0:2], refs[2:4]
    input_ref, qkv_ref, proj_ref = refs[4:7]
    x_all, u_all, w_all, qkv_two, front, d_all, t_all, part_all, landed, early = refs[7:17]
    keep_a, keep_b, send_a, send_b, got_a, got_b, fwd_a, fwd_b, full_a, full_b, last_a, last_b = refs[17:29]
    load_sem, swap_send, swap_recv, ring_send, ring_recv = refs[29:34]
    send_sem, recv_sem, back_send, back_recv, out_send, out_recv = refs[34:40]
    early_send, early_recv, pass_send, pass_recv = refs[40:]
    every = (x_all, u_all)
    tokens, model = given[0].shape
    width = out_weight_ref.shape[1]
    pairs = tokens // n_ctx
    frames = n_ctx // 4
    halved = tokens // 2
    some = early.shape[2]
    half = rows // 2
    dp, ctx, space = (lax.axis_index(name) for name in ("dp", "ctx", "space"))
    x, z, core = (ctx // 2 % 2) * 2 + dp, ctx // 4, ctx % 2

    def peer(dx, dz, dcore):
        px, pz, pc = (x + dx) % 4, (z + dz) % 4, (core + dcore) % 2
        return (px % 2, (pz * 2 + px // 2) * 2 + pc, space)

    def frame_rows(first, count=1):
        return pl.ds(pl.multiple_of(first * pairs, pairs), count * pairs)

    def unit_rows(unit):
        return pl.ds(pl.multiple_of(unit * tokens, tokens), tokens)

    loads = [
        pltpu.make_async_copy(weight_ref, w_all.at[pl.ds(0, 3)], load_sem.at[0]),
        pltpu.make_async_copy(out_weight_ref, w_all.at[3], load_sem.at[1]),
    ]
    for a in range(2):
        mine = frame_rows(ctx)
        loads.append(pltpu.make_async_copy(given[a].at[mine], every[a].at[mine], load_sem.at[2 + a]))
    for load in loads:
        load.start()

    def signal(to):
        pl.semaphore_signal(
            pltpu.get_barrier_semaphore(), inc=1, device_id=to, device_id_type=pl.DeviceIdType.MESH
        )

    def greet(r, carry):
        signal((dp, (ctx + r) % n_ctx, space))
        return carry

    lax.fori_loop(1, n_ctx, greet, 0)
    for d in range(1, n_space):
        signal((dp, ctx, (space + d) % n_space))
    for d in (1, 3):
        signal(peer(d, 0, 0))
    pl.semaphore_wait(pltpu.get_barrier_semaphore(), n_ctx - 1 + n_space - 1 + 2)

    def send(source, target, send_at, recv_at, to):
        return pltpu.make_async_remote_copy(
            src_ref=source,
            dst_ref=target,
            send_sem=send_at,
            recv_sem=recv_at,
            device_id=to,
            device_id_type=pl.DeviceIdType.MESH,
        )

    def swap(a, r):
        to = (ctx + r) % n_ctx
        return send(
            given[a].at[frame_rows(to)],
            every[a].at[frame_rows(ctx)],
            swap_send.at[a, r],
            swap_recv.at[a, r],
            (dp, to, space),
        )

    def arrival(a, r):
        frm = (ctx + n_ctx - r) % n_ctx
        return send(
            given[a].at[frame_rows(frm)],
            every[a].at[frame_rows(frm)],
            swap_send.at[a, r],
            swap_recv.at[a, r],
            (dp, frm, space),
        )

    def beside(way):
        return (dp, ctx, (space + 1 + 2 * way) % n_space)

    def ahead_of_all(way):
        return send(
            given[1].at[:, pl.ds(0, some)],
            early.at[way],
            early_send.at[way],
            early_recv.at[way],
            beside(way),
        )

    def passing(way, r):
        to = (ctx + r) % n_ctx
        return send(
            early.at[way, frame_rows(to)],
            u_all.at[frame_rows((1 + way) * n_ctx + ctx), pl.ds(0, some)],
            pass_send.at[way, r],
            pass_recv.at[way, r],
            (dp, to, space),
        )

    def passed(way, r):
        frm = (ctx + n_ctx - r) % n_ctx
        return send(
            early.at[way, frame_rows(frm)],
            u_all.at[frame_rows((1 + way) * n_ctx + frm), pl.ds(0, some)],
            pass_send.at[way, r],
            pass_recv.at[way, r],
            (dp, frm, space),
        )

    def unpassed(way):
        return pltpu.make_async_copy(
            early.at[way, frame_rows(ctx)],
            u_all.at[frame_rows((1 + way) * n_ctx + ctx), pl.ds(0, some)],
            load_sem.at[5 + way],
        )

    def near(a, h, way):
        at = a * 6 + h * 2 + way
        low = a * some
        return send(
            every[a].at[pl.ds(h * halved, halved), pl.ds(low, model - low)],
            every[a].at[pl.ds((1 + way) * tokens + h * halved, halved), pl.ds(low, model - low)],
            ring_send.at[at],
            ring_recv.at[at],
            beside(way),
        )

    def onward(a, way):
        at = a * 6 + 4 + way
        return send(
            every[a].at[pl.ds((1 + way) * tokens + way * halved, halved)],
            every[a].at[pl.ds(3 * tokens + way * halved, halved)],
            ring_send.at[at],
            ring_recv.at[at],
            beside(way),
        )

    for way in range(2):
        ahead_of_all(way).start()
    for a in range(2):

        def begin(r, carry, a=a):
            swap(a, r).start()
            return carry

        lax.fori_loop(1, n_ctx, begin, 0)

    def spread(a):
        loads[2 + a].wait()
        for h in range(2):

            def settle(frame, carry, a=a):
                r = (ctx + n_ctx - frame) % n_ctx

                @pl.when(r > 0)
                def _():
                    arrival(a, r).wait_recv()

                return carry

            lax.fori_loop(h * n_ctx // 2, (h + 1) * n_ctx // 2, settle, 0)
            for way in range(2):
                near(a, h, way).start()

    def pass_all():
        for way in range(2):
            ahead_of_all(way).wait_recv()
            unpassed(way).start()

            def one(r, carry, way=way):
                passing(way, r).start()
                return carry

            lax.fori_loop(1, n_ctx, one, 0)

    def all_passed():
        for way in range(2):
            unpassed(way).wait()

            def one(r, carry, way=way):
                passed(way, r).wait_recv()
                return carry

            lax.fori_loop(1, n_ctx, one, 0)

    def receive(a):
        for way in range(2):
            near(a, way, way).wait_recv()
            onward(a, way).start()
        for way in range(2):
            near(a, 1 - way, way).wait_recv()

    def group(q):
        return (z + 1 + q) % 4 * frames

    def back(q, which):
        part = frame_rows(group(q), frames)
        return send(
            part_all.at[1 + which, part],
            landed.at[which, part],
            back_send.at[q, which],
            back_recv.at[q, which],
            (dp, ctx, (space + (3, 1, 2)[which]) % n_space),
        )

    def outward(frame):
        return send(
            part_all.at[0, frame_rows(frame)],
            input_ref.at[frame_rows(ctx)],
            out_send.at[frame],
            out_recv.at[ctx],
            (dp, frame, space),
        )

    def inward(frame):
        return send(
            part_all.at[0, frame_rows(frame)],
            input_ref.at[frame_rows(frame)],
            out_send.at[frame],
            out_recv.at[frame],
            (dp, frame, space),
        )

    def kept():
        at = frame_rows(ctx)
        return pltpu.make_async_copy(part_all.at[0, at], input_ref.at[at], load_sem.at[4])

    def quarter(q):
        for which in range(3):
            back(q, which).wait_recv()

        def one(i, carry):
            frame = group(q) + i
            at = frame_rows(frame)
            total = part_all[0, at].astype(F32)
            for which in range(3):
                total += landed[which, at].astype(F32)
            part_all[0, at] = total.astype(BF16)

            @pl.when(frame == ctx)
            def _():
                kept().start()

            @pl.when(frame != ctx)
            def _():
                outward(frame).start()

            return carry

        lax.fori_loop(0, frames, one, 0)

    def project(unit):
        def one(s, carry):
            qkv_two[unit % 2, s] = nn(x_all[unit_rows(unit)], w_all[s]).astype(BF16)
            return carry

        lax.fori_loop(0, 3, one, 0)

    def finish(unit):
        mine = unit_rows(unit)
        front[...] = nn(u_all[mine], w_all[3]).astype(BF16)
        attend_heads(pairs, unit % 2, mine, qkv_two, front, t_all, d_all)
        block = model // 6

        def columns(c, carry):
            at = pl.ds(pl.multiple_of(c * block, block), block)
            total = nt(d_all[mine, 0:width], w_all[0, at, :])
            total += nt(d_all[mine, width : 2 * width], w_all[1, at, :])
            total += nt(d_all[mine, 2 * width :], w_all[2, at, :])
            part_all[unit, :, at] = total.astype(BF16)
            return carry

        lax.fori_loop(0, 6, columns, 0)
        for which in range(3):

            @pl.when(unit == 1 + which)
            def _(which=which):
                for q in range(4):
                    back(q, which).start()

    def step(s, carry):
        pace = (s // 2 + 1) // 2
        unit = pace + (pace % 2) * (s % 2) + pace // 2
        first = (s == 0) | (s == 2) | (s == 3) | (s == 6)

        @pl.when(s == 0)
        def _():
            spread(0)
            pass_all()
            loads[0].wait()
            loads[1].wait()

        @pl.when(s == 1)
        def _():
            spread(1)

        @pl.when(s == 2)
        def _():
            receive(0)

        @pl.when(s == 4)
        def _():
            all_passed()
            receive(1)

        @pl.when(s == 6)
        def _():
            for way in range(2):
                onward(0, way).wait_recv()

        @pl.when(s == 7)
        def _():
            for way in range(2):
                onward(1, way).wait_recv()

        @pl.when(first)
        def _():
            project(unit)

        @pl.when(jnp.logical_not(first))
        def _():
            finish(unit)

        return carry

    lax.fori_loop(0, 8, step, 0)

    def copy(source, target, at, to):
        return send(source, target, send_sem.at[at], recv_sem.at[at], to)

    def far(t):
        k = t // 2
        return t % 2, (2 + k + (k // 2) * (1 + 2 * (k % 2))) % 4

    def trades(t):
        return (
            copy(send_a.at[t % 2], got_a.at[t % 4], 2 * t, peer(0, 0, 1)),
            copy(send_b.at[t % 2], got_b.at[t % 4], 2 * t + 1, peer(0, 0, 1)),
        )

    def forward_a(t, dz, way):
        piece = keep_a.at[t, 1, pl.ds(way * half, half)]
        return copy(piece, fwd_a.at[way, dz], FORWARD_A + 2 * dz + way, peer(1 + 2 * way, 0, 0))

    def full_of_a(t, dz, way):
        return copy(keep_a.at[t, way], full_a.at[way, dz], FULL_A + 2 * dz + way, peer(1 + 2 * way, 0, 0))

    def forward_b(t, dx, hi, way):
        piece = keep_b.at[t, hi, pl.ds(way * half, half)]
        return copy(piece, fwd_b.at[way, dx], FORWARD_B + 2 * dx + way, peer(0, 1 + 2 * way, 0))

    def full_of_b(t, dx, hi, way):
        return copy(keep_b.at[t, hi], full_b.at[way, dx], FULL_B + 2 * dx + way, peer(0, 1 + 2 * way, 0))

    def compute(t):
        p, dz = far(t)
        start = ((x + p) % 4) // 2
        off = 4 * rows * (((dp + p) % 2) * 4 + (z + dz) % 4)
        columns = pl.ds(pl.multiple_of(off, 128), 4 * rows)

        @pl.when(t >= 2)
        def _():
            for trade in trades(t - 2):
                trade.wait_send()

        def put(send_ref, keep_ref, low, total):
            high = low + total.shape[1]
            for hi in range(2):
                spot = (hi + 2 - start) % 2
                even = total[2 * hi * rows : (2 * hi + 1) * rows]
                odd = total[(2 * hi + 1) * rows : (2 * hi + 2) * rows]

                @pl.when(core == 0)
                def _():
                    keep_ref[t, spot, :, low:high] = even
                    send_ref[t % 2, spot, :, low:high] = odd

                @pl.when(core == 1)
                def _():
                    keep_ref[t, spot, :, low:high] = odd
                    send_ref[t % 2, spot, :, low:high] = even

        source = x_all[:, columns]
        put(send_a, keep_a, 0, tn(source, d_all[:, : 2 * width]))
        put(send_b, keep_b, 0, tn(source, d_all[:, 2 * width :]))
        put(send_b, keep_b, width, tn(u_all[:, columns], t_all[...]))
        for trade in trades(t):
            trade.start()

    def pair_up(t):
        p, dz = far(t)
        for trade in trades(t):
            trade.wait_recv()
        keep_a[t] += got_a[t % 4]
        keep_b[t] += got_b[t % 4]

        @pl.when(p == 0)
        def _():
            for way in range(2):
                forward_a(t, dz, way).start()

        @pl.when(dz == 2)
        def _():
            for hi in range(2):
                for way in range(2):
                    forward_b(t, p + 2 * hi, hi, way).start()

    def pass_on(t):
        p, dz = far(t)

        @pl.when(p == 1)
        def _():
            for way in range(2):
                forward_a(t, dz, way).wait_recv()
                keep_a[t, way, pl.ds(way * half, half)] += fwd_a[way, dz]
                full_of_a(t, dz, way).start()

        @pl.when(dz % 2 == 1)
        def _():
            way = dz // 2
            for hi in range(2):
                dx = p + 2 * hi
                forward_b(t, dx, hi, way).wait_recv()
                part = pl.ds(pl.multiple_of(way * half, half), half)
                keep_b[t, hi, part] += fwd_b[way, dx]
                full_of_b(t, dx, hi, way).start()

    def work(t, carry):
        @pl.when(t < 8)
        def _():
            compute(t)

        @pl.when((t >= 1) & (t < 9))
        def _():
            pair_up(t - 1)

        @pl.when(t >= 2)
        def _():
            pass_on(t - 2)

        return carry

    lax.fori_loop(0, 10, work, 0)

    def finish_a(dz):
        t = 2 * RANK[dz]
        for way in range(2):
            full_of_a(t, dz, way).wait_recv()
        keep_a[t, 0] += full_a[0, dz] + full_a[1, dz]

    def finish_b(dx):
        t, hi = 6 + dx % 2, dx // 2
        for way in range(2):
            full_of_b(t, dx, hi, way).wait_recv()
        keep_b[t, hi] += full_b[0, dx] + full_b[1, dx]

    def last_of_a(dz):
        return copy(keep_a.at[2 * RANK[dz], 0], last_a.at[dz - 1], LAST_A + dz - 1, peer(0, dz, 0))

    def last_of_b(dx):
        return copy(keep_b.at[6 + dx % 2, dx // 2], last_b.at[dx - 1], LAST_B + dx - 1, peer(dx, 0, 0))

    quarter(0)
    for d in (2, 3, 1):
        finish_a(d)
        last_of_a(d).start()
        finish_b(d)
        last_of_b(d).start()
    finish_a(0)
    finish_b(0)
    quarter(1)
    quarter(2)
    for d in (2, 3, 1):
        last_of_a(d).wait_recv()
        last_of_b(d).wait_recv()
    sum_a = keep_a[6, 0] + last_a[0] + last_a[1] + last_a[2]
    sum_b = keep_b[6, 0] + last_b[0] + last_b[1] + last_b[2]
    qkv_ref[0] = sum_a[:, :width]
    qkv_ref[1] = sum_a[:, width:]
    qkv_ref[2] = sum_b[:, :width]
    proj_ref[...] = sum_b[:, width:]
    quarter(3)

    def settle(frame, carry):
        @pl.when(frame == ctx)
        def _():
            kept().wait()

        @pl.when(frame != ctx)
        def _():
            outward(frame).wait_send()
            inward(frame).wait_recv()

        return carry

    lax.fori_loop(0, n_ctx, settle, 0)

    def home(q, carry):
        for which in range(3):
            back(q, which).wait_send()
        return carry

    lax.fori_loop(0, 4, home, 0)
    for a in range(2):

        def sent(r, carry, a=a):
            swap(a, r).wait_send()
            return carry

        lax.fori_loop(1, n_ctx, sent, 0)
        for way in range(2):
            for h in range(2):
                near(a, h, way).wait_send()
            onward(a, way).wait_send()
    for way in range(2):
        ahead_of_all(way).wait_send()

        def gone(r, carry, way=way):
            passing(way, r).wait_send()
            return carry

        lax.fori_loop(1, n_ctx, gone, 0)
    for t in (6, 7):
        for trade in trades(t):
            trade.wait_send()

    def drain(t, carry):
        p, dz = far(t)

        @pl.when(p == 0)
        def _():
            for way in range(2):
                forward_a(t, dz, way).wait_send()

        @pl.when(p == 1)
        def _():
            for way in range(2):
                full_of_a(t, dz, way).wait_send()

        @pl.when(dz == 2)
        def _():
            for hi in range(2):
                for way in range(2):
                    forward_b(t, p + 2 * hi, hi, way).wait_send()

        @pl.when(dz % 2 == 1)
        def _():
            for hi in range(2):
                full_of_b(t, p + 2 * hi, hi, dz // 2).wait_send()

        return carry

    lax.fori_loop(0, 8, drain, 0)
    for d in (2, 3, 1):
        last_of_a(d).wait_send()
        last_of_b(d).wait_send()


def whole(n_ctx, n_space, rows, inputs, upstream, qkv_weight, out_weight):
    tokens, model = inputs.shape
    width = out_weight.shape[1]
    wide = 2 * width
    vmem, dma = pltpu.VMEM, pltpu.SemaphoreType.DMA
    return pl.pallas_call(
        lambda *refs: whole_kernel(n_ctx, n_space, rows, *refs),
        out_shape=(
            jax.ShapeDtypeStruct((tokens, model), BF16),
            jax.ShapeDtypeStruct((3, rows, width), F32),
            jax.ShapeDtypeStruct((rows, width), F32),
        ),
        in_specs=[pl.BlockSpec(memory_space=pl.ANY)] * 4,
        out_specs=(pl.BlockSpec(memory_space=pl.ANY),) + (pl.BlockSpec(memory_space=vmem),) * 2,
        scratch_shapes=[
            vmem((4 * tokens, model), BF16),
            vmem((4 * tokens, model), BF16),
            vmem((4, model, width), BF16),
            vmem((2, 3, tokens, width), BF16),
            vmem((tokens, width), BF16),
            vmem((4 * tokens, 3 * width), BF16),
            vmem((4 * tokens, width), BF16),
            vmem((4, tokens, model), BF16),
            vmem((3, tokens, model), BF16),
            vmem((2, tokens, model // 2), BF16),
            vmem((8, 2, rows, wide), F32),
            vmem((8, 2, rows, wide), F32),
            vmem((2, 2, rows, wide), F32),
            vmem((2, 2, rows, wide), F32),
            vmem((4, 2, rows, wide), F32),
            vmem((4, 2, rows, wide), F32),
            vmem((2, 4, rows // 2, wide), F32),
            vmem((2, 4, rows // 2, wide), F32),
            vmem((2, 4, rows, wide), F32),
            vmem((2, 4, rows, wide), F32),
            vmem((3, rows, wide), F32),
            vmem((3, rows, wide), F32),
            dma((7,)),
            dma((2, n_ctx)),
            dma((2, n_ctx)),
            dma((12,)),
            dma((12,)),
            dma((COPIES,)),
            dma((COPIES,)),
            dma((4, 3)),
            dma((4, 3)),
            dma((n_ctx,)),
            dma((n_ctx,)),
            dma((2,)),
            dma((2,)),
            dma((2, n_ctx)),
            dma((2, n_ctx)),
        ],
        compiler_params=pltpu.CompilerParams(
            collective_id=0, has_side_effects=True, vmem_limit_bytes=67043328
        ),
        name="whole",
    )(inputs, upstream, qkv_weight, out_weight)


def solution(mesh):
    n_dp, n_ctx, n_space = mesh.shape["dp"], mesh.shape["ctx"], mesh.shape["space"]

    def body(inputs, upstream, qkv_weight, out_weight):
        clips, single, patches, model = inputs.shape
        tokens = clips * patches
        input_grad, qkv_grad, proj_grad = whole(
            n_ctx,
            n_space,
            model // (n_dp * n_ctx),
            inputs.reshape(tokens, model),
            upstream.reshape(tokens, model),
            qkv_weight,
            out_weight,
        )
        return input_grad.reshape(clips, single, patches, model), qkv_grad, proj_grad

    placed = (
        P("dp", "ctx", "space", None),
        P("dp", "ctx", "space", None),
        P(None, None, "space"),
        P(None, "space"),
    )
    return jax.shard_map(
        body,
        mesh=mesh,
        in_specs=placed,
        out_specs=(
            P("dp", "ctx", "space", None),
            P(None, ("dp", "ctx"), "space"),
            P(("dp", "ctx"), "space"),
        ),
        check_vma=False,
    )
```

```python
import math

import jax
import jax.numpy as jnp
from jax import lax
from jax.experimental import pallas as pl
from jax.experimental.pallas import tpu as pltpu
from jax.sharding import PartitionSpec as P

HS = 128
F32 = jnp.float32
BF16 = jnp.bfloat16


def nn(a, b):
    return lax.dot_general(a, b, (((1,), (0,)), ((), ())), preferred_element_type=F32)


def nt(a, b):
    return lax.dot_general(a, b, (((1,), (1,)), ((), ())), preferred_element_type=F32)


def tn(a, b):
    return lax.dot_general(a, b, (((0,), (0,)), ((), ())), preferred_element_type=F32)


def attend_heads(pairs, slot, mine, qkv_ref, front_ref, att_ref, dqkv_ref):
    tokens, width = front_ref.shape
    scale = 1.0 / math.sqrt(HS)
    row = lax.broadcasted_iota(jnp.int32, (tokens, tokens), 0)
    col = lax.broadcasted_iota(jnp.int32, (tokens, tokens), 1)
    valid = (row >= col) & (row % pairs == col % pairs)
    for head in range(width // HS):
        cols = slice(head * HS, (head + 1) * HS)
        k_cols = slice(width + head * HS, width + (head + 1) * HS)
        v_cols = slice(2 * width + head * HS, 2 * width + (head + 1) * HS)
        query, key, value = (qkv_ref[slot, s, :, cols] for s in range(3))
        front = front_ref[:, cols]
        masked = jnp.where(valid, nt(query, key) * scale, F32(-1e30))
        top = jnp.max(masked, axis=-1, keepdims=True)
        expo = jnp.where(valid, jnp.exp(masked - top), F32(0.0))
        probs = expo / jnp.sum(expo, axis=-1, keepdims=True)
        probs_b = probs.astype(BF16)
        att_ref[mine, cols] = nn(probs_b, value).astype(BF16)
        dprobs = nt(front, value)
        dqkv_ref[mine, v_cols] = tn(probs_b, front).astype(BF16)
        weighed = probs * dprobs
        dscore = probs * (dprobs - jnp.sum(weighed, axis=-1, keepdims=True))
        dscore_b = dscore.astype(BF16)
        dqkv_ref[mine, cols] = (nn(dscore_b, key) * scale).astype(BF16)
        dqkv_ref[mine, k_cols] = (tn(dscore_b, query) * scale).astype(BF16)


FORWARD_A, FULL_A, FORWARD_B, FULL_B, LAST_A, LAST_B = 16, 24, 32, 40, 48, 51
COPIES = 54
RANK = {2: 0, 3: 1, 1: 2, 0: 3}


def whole_kernel(n_ctx, n_space, rows, *refs):
    given, (weight_ref, out_weight_ref) = refs[0:2], refs[2:4]
    input_ref, qkv_ref, proj_ref = refs[4:7]
    x_all, u_all, w_all, qkv_two, front, d_all, t_all, part_all, landed, early = refs[7:17]
    keep_a, keep_b, send_a, send_b, got_a, got_b, fwd_a, fwd_b, full_a, full_b, last_a, last_b = refs[17:29]
    load_sem, swap_send, swap_recv, ring_send, ring_recv = refs[29:34]
    send_sem, recv_sem, back_send, back_recv, out_send, out_recv = refs[34:40]
    early_send, early_recv, pass_send, pass_recv = refs[40:]
    every = (x_all, u_all)
    tokens, model = given[0].shape
    width = out_weight_ref.shape[1]
    pairs = tokens // n_ctx
    frames = n_ctx // 4
    halved = tokens // 2
    some = early.shape[2]
    half = rows // 2
    dp, ctx, space = (lax.axis_index(name) for name in ("dp", "ctx", "space"))
    x, z, core = (ctx // 2 % 2) * 2 + dp, ctx // 4, ctx % 2

    def peer(dx, dz, dcore):
        px, pz, pc = (x + dx) % 4, (z + dz) % 4, (core + dcore) % 2
        return (px % 2, (pz * 2 + px // 2) * 2 + pc, space)

    def frame_rows(first, count=1):
        return pl.ds(pl.multiple_of(first * pairs, pairs), count * pairs)

    def unit_rows(unit):
        return pl.ds(pl.multiple_of(unit * tokens, tokens), tokens)

    loads = [
        pltpu.make_async_copy(weight_ref, w_all.at[pl.ds(0, 3)], load_sem.at[0]),
        pltpu.make_async_copy(out_weight_ref, w_all.at[3], load_sem.at[1]),
    ]
    for a in range(2):
        mine = frame_rows(ctx)
        loads.append(pltpu.make_async_copy(given[a].at[mine], every[a].at[mine], load_sem.at[2 + a]))
    for load in loads:
        load.start()

    def signal(to):
        pl.semaphore_signal(
            pltpu.get_barrier_semaphore(), inc=1, device_id=to, device_id_type=pl.DeviceIdType.MESH
        )

    def greet(r, carry):
        signal((dp, (ctx + r) % n_ctx, space))
        return carry

    lax.fori_loop(1, n_ctx, greet, 0)
    for d in range(1, n_space):
        signal((dp, ctx, (space + d) % n_space))
    for d in (1, 3):
        signal(peer(d, 0, 0))
    pl.semaphore_wait(pltpu.get_barrier_semaphore(), n_ctx - 1 + n_space - 1 + 2)

    def send(source, target, send_at, recv_at, to):
        return pltpu.make_async_remote_copy(
            src_ref=source,
            dst_ref=target,
            send_sem=send_at,
            recv_sem=recv_at,
            device_id=to,
            device_id_type=pl.DeviceIdType.MESH,
        )

    def swap(a, r):
        to = (ctx + r) % n_ctx
        return send(
            given[a].at[frame_rows(to)],
            every[a].at[frame_rows(ctx)],
            swap_send.at[a, r],
            swap_recv.at[a, r],
            (dp, to, space),
        )

    def arrival(a, r):
        frm = (ctx + n_ctx - r) % n_ctx
        return send(
            given[a].at[frame_rows(frm)],
            every[a].at[frame_rows(frm)],
            swap_send.at[a, r],
            swap_recv.at[a, r],
            (dp, frm, space),
        )

    def beside(way):
        return (dp, ctx, (space + 1 + 2 * way) % n_space)

    def ahead_of_all(way):
        return send(
            given[1].at[:, pl.ds(0, some)],
            early.at[way],
            early_send.at[way],
            early_recv.at[way],
            beside(way),
        )

    def passing(way, r):
        to = (ctx + r) % n_ctx
        return send(
            early.at[way, frame_rows(to)],
            u_all.at[frame_rows((1 + way) * n_ctx + ctx), pl.ds(0, some)],
            pass_send.at[way, r],
            pass_recv.at[way, r],
            (dp, to, space),
        )

    def passed(way, r):
        frm = (ctx + n_ctx - r) % n_ctx
        return send(
            early.at[way, frame_rows(frm)],
            u_all.at[frame_rows((1 + way) * n_ctx + frm), pl.ds(0, some)],
            pass_send.at[way, r],
            pass_recv.at[way, r],
            (dp, frm, space),
        )

    def unpassed(way):
        return pltpu.make_async_copy(
            early.at[way, frame_rows(ctx)],
            u_all.at[frame_rows((1 + way) * n_ctx + ctx), pl.ds(0, some)],
            load_sem.at[5 + way],
        )

    def near(a, h, way):
        at = a * 6 + h * 2 + way
        low = a * some
        return send(
            every[a].at[pl.ds(h * halved, halved), pl.ds(low, model - low)],
            every[a].at[pl.ds((1 + way) * tokens + h * halved, halved), pl.ds(low, model - low)],
            ring_send.at[at],
            ring_recv.at[at],
            beside(way),
        )

    def onward(a, way):
        at = a * 6 + 4 + way
        return send(
            every[a].at[pl.ds((1 + way) * tokens + way * halved, halved)],
            every[a].at[pl.ds(3 * tokens + way * halved, halved)],
            ring_send.at[at],
            ring_recv.at[at],
            beside(way),
        )

    for way in range(2):
        ahead_of_all(way).start()
    for a in range(2):

        def begin(r, carry, a=a):
            swap(a, r).start()
            return carry

        lax.fori_loop(1, n_ctx, begin, 0)

    def spread(a):
        loads[2 + a].wait()
        for h in range(2):

            def settle(frame, carry, a=a):
                r = (ctx + n_ctx - frame) % n_ctx

                @pl.when(r > 0)
                def _():
                    arrival(a, r).wait_recv()

                return carry

            lax.fori_loop(h * n_ctx // 2, (h + 1) * n_ctx // 2, settle, 0)
            for way in range(2):
                near(a, h, way).start()

    def pass_all():
        for way in range(2):
            ahead_of_all(way).wait_recv()
            unpassed(way).start()

            def one(r, carry, way=way):
                passing(way, r).start()
                return carry

            lax.fori_loop(1, n_ctx, one, 0)

    def all_passed():
        for way in range(2):
            unpassed(way).wait()

            def one(r, carry, way=way):
                passed(way, r).wait_recv()
                return carry

            lax.fori_loop(1, n_ctx, one, 0)

    def receive(a):
        for way in range(2):
            near(a, way, way).wait_recv()
            onward(a, way).start()
        for way in range(2):
            near(a, 1 - way, way).wait_recv()

    def group(q):
        return (z + 1 + q) % 4 * frames

    def back(q, which):
        part = frame_rows(group(q), frames)
        return send(
            part_all.at[1 + which, part],
            landed.at[which, part],
            back_send.at[q, which],
            back_recv.at[q, which],
            (dp, ctx, (space + (3, 1, 2)[which]) % n_space),
        )

    def outward(frame):
        return send(
            part_all.at[0, frame_rows(frame)],
            input_ref.at[frame_rows(ctx)],
            out_send.at[frame],
            out_recv.at[ctx],
            (dp, frame, space),
        )

    def inward(frame):
        return send(
            part_all.at[0, frame_rows(frame)],
            input_ref.at[frame_rows(frame)],
            out_send.at[frame],
            out_recv.at[frame],
            (dp, frame, space),
        )

    def kept():
        at = frame_rows(ctx)
        return pltpu.make_async_copy(part_all.at[0, at], input_ref.at[at], load_sem.at[4])

    def quarter(q):
        for which in range(3):
            back(q, which).wait_recv()

        def one(i, carry):
            frame = group(q) + i
            at = frame_rows(frame)
            total = part_all[0, at].astype(F32)
            for which in range(3):
                total += landed[which, at].astype(F32)
            part_all[0, at] = total.astype(BF16)

            @pl.when(frame == ctx)
            def _():
                kept().start()

            @pl.when(frame != ctx)
            def _():
                outward(frame).start()

            return carry

        lax.fori_loop(0, frames, one, 0)

    def project(unit):
        def one(s, carry):
            qkv_two[unit % 2, s] = nn(x_all[unit_rows(unit)], w_all[s]).astype(BF16)
            return carry

        lax.fori_loop(0, 3, one, 0)

    def finish(unit):
        mine = unit_rows(unit)
        front[...] = nn(u_all[mine], w_all[3]).astype(BF16)
        attend_heads(pairs, unit % 2, mine, qkv_two, front, t_all, d_all)

    def give_back(unit):
        mine = unit_rows(unit)
        block = model // 6

        def columns(c, carry):
            at = pl.ds(pl.multiple_of(c * block, block), block)
            total = nt(d_all[mine, 0:width], w_all[0, at, :])
            total += nt(d_all[mine, width : 2 * width], w_all[1, at, :])
            total += nt(d_all[mine, 2 * width :], w_all[2, at, :])
            part_all[unit, :, at] = total.astype(BF16)
            return carry

        lax.fori_loop(0, 6, columns, 0)
        for which in range(3):

            @pl.when(unit == 1 + which)
            def _(which=which):
                for q in range(4):
                    back(q, which).start()

    def step(s, carry):
        pace = (s // 2 + 1) // 2
        unit = pace + (pace % 2) * (s % 2) + pace // 2
        first = (s == 0) | (s == 2) | (s == 3) | (s == 6)

        @pl.when(s == 0)
        def _():
            spread(0)
            pass_all()
            loads[0].wait()
            loads[1].wait()

        @pl.when(s == 1)
        def _():
            spread(1)

        @pl.when(s == 2)
        def _():
            receive(0)

        @pl.when(s == 4)
        def _():
            all_passed()
            receive(1)

        @pl.when(s == 6)
        def _():
            for way in range(2):
                onward(0, way).wait_recv()

        @pl.when(s == 7)
        def _():
            for way in range(2):
                onward(1, way).wait_recv()

        @pl.when(first)
        def _():
            project(unit)

        @pl.when(jnp.logical_not(first))
        def _():
            finish(unit)

        @pl.when(jnp.logical_not(first) & (unit < 3))
        def _():
            give_back(unit)

        return carry

    lax.fori_loop(0, 8, step, 0)

    def copy(source, target, at, to):
        return send(source, target, send_sem.at[at], recv_sem.at[at], to)

    def far(t):
        k = t // 2
        return t % 2, (2 + k + (k // 2) * (1 + 2 * (k % 2))) % 4

    def trades(t):
        return (
            copy(send_a.at[t % 2], got_a.at[t % 4], 2 * t, peer(0, 0, 1)),
            copy(send_b.at[t % 2], got_b.at[t % 4], 2 * t + 1, peer(0, 0, 1)),
        )

    def forward_a(t, dz, way):
        piece = keep_a.at[t, 1, pl.ds(way * half, half)]
        return copy(piece, fwd_a.at[way, dz], FORWARD_A + 2 * dz + way, peer(1 + 2 * way, 0, 0))

    def full_of_a(t, dz, way):
        return copy(keep_a.at[t, way], full_a.at[way, dz], FULL_A + 2 * dz + way, peer(1 + 2 * way, 0, 0))

    def forward_b(t, dx, hi, way):
        piece = keep_b.at[t, hi, pl.ds(way * half, half)]
        return copy(piece, fwd_b.at[way, dx], FORWARD_B + 2 * dx + way, peer(0, 1 + 2 * way, 0))

    def full_of_b(t, dx, hi, way):
        return copy(keep_b.at[t, hi], full_b.at[way, dx], FULL_B + 2 * dx + way, peer(0, 1 + 2 * way, 0))

    def compute(t):
        p, dz = far(t)
        start = ((x + p) % 4) // 2
        off = 4 * rows * (((dp + p) % 2) * 4 + (z + dz) % 4)
        columns = pl.ds(pl.multiple_of(off, 128), 4 * rows)

        @pl.when(t >= 2)
        def _():
            for trade in trades(t - 2):
                trade.wait_send()

        def put(send_ref, keep_ref, low, total):
            high = low + total.shape[1]
            for hi in range(2):
                spot = (hi + 2 - start) % 2
                even = total[2 * hi * rows : (2 * hi + 1) * rows]
                odd = total[(2 * hi + 1) * rows : (2 * hi + 2) * rows]

                @pl.when(core == 0)
                def _():
                    keep_ref[t, spot, :, low:high] = even
                    send_ref[t % 2, spot, :, low:high] = odd

                @pl.when(core == 1)
                def _():
                    keep_ref[t, spot, :, low:high] = odd
                    send_ref[t % 2, spot, :, low:high] = even

        source = x_all[:, columns]
        put(send_a, keep_a, 0, tn(source, d_all[:, : 2 * width]))
        put(send_b, keep_b, 0, tn(source, d_all[:, 2 * width :]))
        put(send_b, keep_b, width, tn(u_all[:, columns], t_all[...]))
        for trade in trades(t):
            trade.start()

    def pair_up(t):
        p, dz = far(t)
        for trade in trades(t):
            trade.wait_recv()
        keep_a[t] += got_a[t % 4]
        keep_b[t] += got_b[t % 4]

        @pl.when(p == 0)
        def _():
            for way in range(2):
                forward_a(t, dz, way).start()

        @pl.when(dz == 2)
        def _():
            for hi in range(2):
                for way in range(2):
                    forward_b(t, p + 2 * hi, hi, way).start()

    def pass_on(t):
        p, dz = far(t)

        @pl.when(p == 1)
        def _():
            for way in range(2):
                forward_a(t, dz, way).wait_recv()
                keep_a[t, way, pl.ds(way * half, half)] += fwd_a[way, dz]
                full_of_a(t, dz, way).start()

        @pl.when(dz % 2 == 1)
        def _():
            way = dz // 2
            for hi in range(2):
                dx = p + 2 * hi
                forward_b(t, dx, hi, way).wait_recv()
                part = pl.ds(pl.multiple_of(way * half, half), half)
                keep_b[t, hi, part] += fwd_b[way, dx]
                full_of_b(t, dx, hi, way).start()

    def work(t, carry):
        @pl.when(t == 1)
        def _():
            give_back(3)

        @pl.when(t < 8)
        def _():
            compute(t)

        @pl.when((t >= 1) & (t < 9))
        def _():
            pair_up(t - 1)

        @pl.when(t >= 2)
        def _():
            pass_on(t - 2)

        return carry

    lax.fori_loop(0, 10, work, 0)

    def finish_a(dz):
        t = 2 * RANK[dz]
        for way in range(2):
            full_of_a(t, dz, way).wait_recv()
        keep_a[t, 0] += full_a[0, dz] + full_a[1, dz]

    def finish_b(dx):
        t, hi = 6 + dx % 2, dx // 2
        for way in range(2):
            full_of_b(t, dx, hi, way).wait_recv()
        keep_b[t, hi] += full_b[0, dx] + full_b[1, dx]

    def last_of_a(dz):
        return copy(keep_a.at[2 * RANK[dz], 0], last_a.at[dz - 1], LAST_A + dz - 1, peer(0, dz, 0))

    def last_of_b(dx):
        return copy(keep_b.at[6 + dx % 2, dx // 2], last_b.at[dx - 1], LAST_B + dx - 1, peer(dx, 0, 0))

    for d in (2, 3, 1):
        finish_a(d)
        last_of_a(d).start()
        finish_b(d)
        last_of_b(d).start()
    finish_a(0)
    finish_b(0)
    quarter(0)
    quarter(1)
    quarter(2)
    for d in (2, 3, 1):
        last_of_a(d).wait_recv()
        last_of_b(d).wait_recv()
    sum_a = keep_a[6, 0] + last_a[0] + last_a[1] + last_a[2]
    sum_b = keep_b[6, 0] + last_b[0] + last_b[1] + last_b[2]
    qkv_ref[0] = sum_a[:, :width]
    qkv_ref[1] = sum_a[:, width:]
    qkv_ref[2] = sum_b[:, :width]
    proj_ref[...] = sum_b[:, width:]
    quarter(3)

    def settle(frame, carry):
        @pl.when(frame == ctx)
        def _():
            kept().wait()

        @pl.when(frame != ctx)
        def _():
            outward(frame).wait_send()
            inward(frame).wait_recv()

        return carry

    lax.fori_loop(0, n_ctx, settle, 0)

    def home(q, carry):
        for which in range(3):
            back(q, which).wait_send()
        return carry

    lax.fori_loop(0, 4, home, 0)
    for a in range(2):

        def sent(r, carry, a=a):
            swap(a, r).wait_send()
            return carry

        lax.fori_loop(1, n_ctx, sent, 0)
        for way in range(2):
            for h in range(2):
                near(a, h, way).wait_send()
            onward(a, way).wait_send()
    for way in range(2):
        ahead_of_all(way).wait_send()

        def gone(r, carry, way=way):
            passing(way, r).wait_send()
            return carry

        lax.fori_loop(1, n_ctx, gone, 0)
    for t in (6, 7):
        for trade in trades(t):
            trade.wait_send()

    def drain(t, carry):
        p, dz = far(t)

        @pl.when(p == 0)
        def _():
            for way in range(2):
                forward_a(t, dz, way).wait_send()

        @pl.when(p == 1)
        def _():
            for way in range(2):
                full_of_a(t, dz, way).wait_send()

        @pl.when(dz == 2)
        def _():
            for hi in range(2):
                for way in range(2):
                    forward_b(t, p + 2 * hi, hi, way).wait_send()

        @pl.when(dz % 2 == 1)
        def _():
            for hi in range(2):
                full_of_b(t, p + 2 * hi, hi, dz // 2).wait_send()

        return carry

    lax.fori_loop(0, 8, drain, 0)
    for d in (2, 3, 1):
        last_of_a(d).wait_send()
        last_of_b(d).wait_send()


def whole(n_ctx, n_space, rows, inputs, upstream, qkv_weight, out_weight):
    tokens, model = inputs.shape
    width = out_weight.shape[1]
    wide = 2 * width
    vmem, dma = pltpu.VMEM, pltpu.SemaphoreType.DMA
    return pl.pallas_call(
        lambda *refs: whole_kernel(n_ctx, n_space, rows, *refs),
        out_shape=(
            jax.ShapeDtypeStruct((tokens, model), BF16),
            jax.ShapeDtypeStruct((3, rows, width), F32),
            jax.ShapeDtypeStruct((rows, width), F32),
        ),
        in_specs=[pl.BlockSpec(memory_space=pl.ANY)] * 4,
        out_specs=(pl.BlockSpec(memory_space=pl.ANY),) + (pl.BlockSpec(memory_space=vmem),) * 2,
        scratch_shapes=[
            vmem((4 * tokens, model), BF16),
            vmem((4 * tokens, model), BF16),
            vmem((4, model, width), BF16),
            vmem((2, 3, tokens, width), BF16),
            vmem((tokens, width), BF16),
            vmem((4 * tokens, 3 * width), BF16),
            vmem((4 * tokens, width), BF16),
            vmem((4, tokens, model), BF16),
            vmem((3, tokens, model), BF16),
            vmem((2, tokens, model // 2), BF16),
            vmem((8, 2, rows, wide), F32),
            vmem((8, 2, rows, wide), F32),
            vmem((2, 2, rows, wide), F32),
            vmem((2, 2, rows, wide), F32),
            vmem((4, 2, rows, wide), F32),
            vmem((4, 2, rows, wide), F32),
            vmem((2, 4, rows // 2, wide), F32),
            vmem((2, 4, rows // 2, wide), F32),
            vmem((2, 4, rows, wide), F32),
            vmem((2, 4, rows, wide), F32),
            vmem((3, rows, wide), F32),
            vmem((3, rows, wide), F32),
            dma((7,)),
            dma((2, n_ctx)),
            dma((2, n_ctx)),
            dma((12,)),
            dma((12,)),
            dma((COPIES,)),
            dma((COPIES,)),
            dma((4, 3)),
            dma((4, 3)),
            dma((n_ctx,)),
            dma((n_ctx,)),
            dma((2,)),
            dma((2,)),
            dma((2, n_ctx)),
            dma((2, n_ctx)),
        ],
        compiler_params=pltpu.CompilerParams(
            collective_id=0, has_side_effects=True, vmem_limit_bytes=67043328
        ),
        name="whole",
    )(inputs, upstream, qkv_weight, out_weight)


def solution(mesh):
    n_dp, n_ctx, n_space = mesh.shape["dp"], mesh.shape["ctx"], mesh.shape["space"]

    def body(inputs, upstream, qkv_weight, out_weight):
        clips, single, patches, model = inputs.shape
        tokens = clips * patches
        input_grad, qkv_grad, proj_grad = whole(
            n_ctx,
            n_space,
            model // (n_dp * n_ctx),
            inputs.reshape(tokens, model),
            upstream.reshape(tokens, model),
            qkv_weight,
            out_weight,
        )
        return input_grad.reshape(clips, single, patches, model), qkv_grad, proj_grad

    placed = (
        P("dp", "ctx", "space", None),
        P("dp", "ctx", "space", None),
        P(None, None, "space"),
        P(None, "space"),
    )
    return jax.shard_map(
        body,
        mesh=mesh,
        in_specs=placed,
        out_specs=(
            P("dp", "ctx", "space", None),
            P(None, ("dp", "ctx"), "space"),
            P(("dp", "ctx"), "space"),
        ),
        check_vma=False,
    )
```

```python
import math

import jax
import jax.numpy as jnp
from jax import lax
from jax.experimental import pallas as pl
from jax.experimental.pallas import tpu as pltpu
from jax.sharding import PartitionSpec as P

HS = 128
F32 = jnp.float32
BF16 = jnp.bfloat16


def nn(a, b):
    return lax.dot_general(a, b, (((1,), (0,)), ((), ())), preferred_element_type=F32)


def nt(a, b):
    return lax.dot_general(a, b, (((1,), (1,)), ((), ())), preferred_element_type=F32)


def tn(a, b):
    return lax.dot_general(a, b, (((0,), (0,)), ((), ())), preferred_element_type=F32)


def attend_heads(pairs, slot, mine, qkv_ref, att_ref, dqkv_ref):
    tokens, width = qkv_ref.shape[2:]
    scale = 1.0 / math.sqrt(HS)
    row = lax.broadcasted_iota(jnp.int32, (tokens, tokens), 0)
    col = lax.broadcasted_iota(jnp.int32, (tokens, tokens), 1)
    valid = (row >= col) & (row % pairs == col % pairs)
    for head in range(width // HS):
        cols = slice(head * HS, (head + 1) * HS)
        k_cols = slice(width + head * HS, width + (head + 1) * HS)
        v_cols = slice(2 * width + head * HS, 2 * width + (head + 1) * HS)
        query, key, value = (qkv_ref[slot, s, :, cols] for s in range(3))
        front = att_ref[mine, cols]
        masked = jnp.where(valid, nt(query, key) * scale, F32(-1e30))
        top = jnp.max(masked, axis=-1, keepdims=True)
        expo = jnp.where(valid, jnp.exp(masked - top), F32(0.0))
        probs = expo / jnp.sum(expo, axis=-1, keepdims=True)
        probs_b = probs.astype(BF16)
        att_ref[mine, cols] = nn(probs_b, value).astype(BF16)
        dprobs = nt(front, value)
        dqkv_ref[mine, v_cols] = tn(probs_b, front).astype(BF16)
        weighed = probs * dprobs
        dscore = probs * (dprobs - jnp.sum(weighed, axis=-1, keepdims=True))
        dscore_b = dscore.astype(BF16)
        dqkv_ref[mine, cols] = (nn(dscore_b, key) * scale).astype(BF16)
        dqkv_ref[mine, k_cols] = (tn(dscore_b, query) * scale).astype(BF16)


FORWARD_A, FULL_A, FORWARD_B, FULL_B, LAST_A, LAST_B = 16, 24, 32, 40, 48, 51
COPIES = 54
RANK = {2: 0, 3: 1, 1: 2, 0: 3}


def whole_kernel(n_ctx, n_space, rows, *refs):
    given, (weight_ref, out_weight_ref) = refs[0:2], refs[2:4]
    input_ref, qkv_ref, proj_ref = refs[4:7]
    x_all, u_all, w_all, qkv_two, d_all, t_all, part_all, landed, early = refs[7:16]
    keep_a, keep_b, send_a, send_b, got_a, got_b, fwd_a, fwd_b, full_a, full_b, last_a, last_b = refs[16:28]
    load_sem, swap_send, swap_recv, ring_send, ring_recv = refs[28:33]
    send_sem, recv_sem, back_send, back_recv, out_send, out_recv = refs[33:39]
    early_send, early_recv, pass_send, pass_recv = refs[39:]
    every = (x_all, u_all)
    tokens, model = given[0].shape
    width = out_weight_ref.shape[1]
    pairs = tokens // n_ctx
    frames = n_ctx // 4
    halved = tokens // 2
    some = early.shape[2]
    half = rows // 2
    dp, ctx, space = (lax.axis_index(name) for name in ("dp", "ctx", "space"))
    x, z, core = (ctx // 2 % 2) * 2 + dp, ctx // 4, ctx % 2

    def peer(dx, dz, dcore):
        px, pz, pc = (x + dx) % 4, (z + dz) % 4, (core + dcore) % 2
        return (px % 2, (pz * 2 + px // 2) * 2 + pc, space)

    def frame_rows(first, count=1):
        return pl.ds(pl.multiple_of(first * pairs, pairs), count * pairs)

    def unit_rows(unit):
        return pl.ds(pl.multiple_of(unit * tokens, tokens), tokens)

    loads = [
        pltpu.make_async_copy(weight_ref, w_all.at[pl.ds(0, 3)], load_sem.at[0]),
        pltpu.make_async_copy(out_weight_ref, w_all.at[3], load_sem.at[1]),
    ]
    for a in range(2):
        mine = frame_rows(ctx)
        loads.append(pltpu.make_async_copy(given[a].at[mine], every[a].at[mine], load_sem.at[2 + a]))
    for load in loads:
        load.start()

    def signal(to):
        pl.semaphore_signal(
            pltpu.get_barrier_semaphore(), inc=1, device_id=to, device_id_type=pl.DeviceIdType.MESH
        )

    def greet(r, carry):
        signal((dp, (ctx + r) % n_ctx, space))
        return carry

    lax.fori_loop(1, n_ctx, greet, 0)
    for d in range(1, n_space):
        signal((dp, ctx, (space + d) % n_space))
    for d in (1, 3):
        signal(peer(d, 0, 0))
    pl.semaphore_wait(pltpu.get_barrier_semaphore(), n_ctx - 1 + n_space - 1 + 2)

    def send(source, target, send_at, recv_at, to):
        return pltpu.make_async_remote_copy(
            src_ref=source,
            dst_ref=target,
            send_sem=send_at,
            recv_sem=recv_at,
            device_id=to,
            device_id_type=pl.DeviceIdType.MESH,
        )

    def swap(a, r):
        to = (ctx + r) % n_ctx
        return send(
            given[a].at[frame_rows(to)],
            every[a].at[frame_rows(ctx)],
            swap_send.at[a, r],
            swap_recv.at[a, r],
            (dp, to, space),
        )

    def arrival(a, r):
        frm = (ctx + n_ctx - r) % n_ctx
        return send(
            given[a].at[frame_rows(frm)],
            every[a].at[frame_rows(frm)],
            swap_send.at[a, r],
            swap_recv.at[a, r],
            (dp, frm, space),
        )

    def beside(way):
        return (dp, ctx, (space + 1 + 2 * way) % n_space)

    def ahead_of_all(way):
        return send(
            given[1].at[:, pl.ds(0, some)],
            early.at[way],
            early_send.at[way],
            early_recv.at[way],
            beside(way),
        )

    def passing(way, r):
        to = (ctx + r) % n_ctx
        return send(
            early.at[way, frame_rows(to)],
            u_all.at[frame_rows((1 + way) * n_ctx + ctx), pl.ds(0, some)],
            pass_send.at[way, r],
            pass_recv.at[way, r],
            (dp, to, space),
        )

    def passed(way, r):
        frm = (ctx + n_ctx - r) % n_ctx
        return send(
            early.at[way, frame_rows(frm)],
            u_all.at[frame_rows((1 + way) * n_ctx + frm), pl.ds(0, some)],
            pass_send.at[way, r],
            pass_recv.at[way, r],
            (dp, frm, space),
        )

    def unpassed(way):
        return pltpu.make_async_copy(
            early.at[way, frame_rows(ctx)],
            u_all.at[frame_rows((1 + way) * n_ctx + ctx), pl.ds(0, some)],
            load_sem.at[5 + way],
        )

    def near(a, h, way):
        at = a * 6 + h * 2 + way
        low = a * some
        return send(
            every[a].at[pl.ds(h * halved, halved), pl.ds(low, model - low)],
            every[a].at[pl.ds((1 + way) * tokens + h * halved, halved), pl.ds(low, model - low)],
            ring_send.at[at],
            ring_recv.at[at],
            beside(way),
        )

    def onward(a, way):
        at = a * 6 + 4 + way
        return send(
            every[a].at[pl.ds((1 + way) * tokens + way * halved, halved)],
            every[a].at[pl.ds(3 * tokens + way * halved, halved)],
            ring_send.at[at],
            ring_recv.at[at],
            beside(way),
        )

    for way in range(2):
        ahead_of_all(way).start()
    for a in range(2):

        def begin(r, carry, a=a):
            swap(a, r).start()
            return carry

        lax.fori_loop(1, n_ctx, begin, 0)

    def spread(a):
        loads[2 + a].wait()
        for h in range(2):

            def settle(frame, carry, a=a):
                r = (ctx + n_ctx - frame) % n_ctx

                @pl.when(r > 0)
                def _():
                    arrival(a, r).wait_recv()

                return carry

            lax.fori_loop(h * n_ctx // 2, (h + 1) * n_ctx // 2, settle, 0)
            for way in range(2):
                near(a, h, way).start()

    def pass_all():
        for way in range(2):
            ahead_of_all(way).wait_recv()
            unpassed(way).start()

            def one(r, carry, way=way):
                passing(way, r).start()
                return carry

            lax.fori_loop(1, n_ctx, one, 0)

    def all_passed():
        for way in range(2):
            unpassed(way).wait()

            def one(r, carry, way=way):
                passed(way, r).wait_recv()
                return carry

            lax.fori_loop(1, n_ctx, one, 0)

    def receive(a):
        for way in range(2):
            near(a, way, way).wait_recv()
            onward(a, way).start()
        for way in range(2):
            near(a, 1 - way, way).wait_recv()

    def group(q):
        return (z + 1 + q) % 4 * frames

    def back(q, which):
        part = frame_rows(group(q), frames)
        return send(
            part_all.at[1 + which, part],
            landed.at[which, part],
            back_send.at[q, which],
            back_recv.at[q, which],
            (dp, ctx, (space + (3, 1, 2)[which]) % n_space),
        )

    def outward(frame):
        return send(
            part_all.at[0, frame_rows(frame)],
            input_ref.at[frame_rows(ctx)],
            out_send.at[frame],
            out_recv.at[ctx],
            (dp, frame, space),
        )

    def inward(frame):
        return send(
            part_all.at[0, frame_rows(frame)],
            input_ref.at[frame_rows(frame)],
            out_send.at[frame],
            out_recv.at[frame],
            (dp, frame, space),
        )

    def kept():
        at = frame_rows(ctx)
        return pltpu.make_async_copy(part_all.at[0, at], input_ref.at[at], load_sem.at[4])

    def quarter(q):
        for which in range(3):
            back(q, which).wait_recv()

        def one(i, carry):
            frame = group(q) + i
            at = frame_rows(frame)
            total = part_all[0, at].astype(F32)
            for which in range(3):
                total += landed[which, at].astype(F32)
            part_all[0, at] = total.astype(BF16)

            @pl.when(frame == ctx)
            def _():
                kept().start()

            @pl.when(frame != ctx)
            def _():
                outward(frame).start()

            return carry

        lax.fori_loop(0, frames, one, 0)

    def project(unit):
        def one(s, carry):
            qkv_two[unit % 2, s] = nn(x_all[unit_rows(unit)], w_all[s]).astype(BF16)
            return carry

        lax.fori_loop(0, 3, one, 0)

    def finish(unit):
        mine = unit_rows(unit)
        t_all[mine] = nn(u_all[mine], w_all[3]).astype(BF16)
        attend_heads(pairs, unit % 2, mine, qkv_two, t_all, d_all)

    def give_back(unit):
        mine = unit_rows(unit)
        block = model // 6

        def columns(c, carry):
            at = pl.ds(pl.multiple_of(c * block, block), block)
            total = nt(d_all[mine, 0:width], w_all[0, at, :])
            total += nt(d_all[mine, width : 2 * width], w_all[1, at, :])
            total += nt(d_all[mine, 2 * width :], w_all[2, at, :])
            part_all[unit, :, at] = total.astype(BF16)
            return carry

        lax.fori_loop(0, 6, columns, 0)
        for which in range(3):

            @pl.when(unit == 1 + which)
            def _(which=which):
                for q in range(4):
                    back(q, which).start()

    def step(s, carry):
        pace = (s // 2 + 1) // 2
        unit = pace + (pace % 2) * (s % 2) + pace // 2
        first = (s == 0) | (s == 2) | (s == 3) | (s == 6)

        @pl.when(s == 0)
        def _():
            spread(0)
            pass_all()
            loads[0].wait()
            loads[1].wait()

        @pl.when(s == 1)
        def _():
            spread(1)

        @pl.when(s == 2)
        def _():
            receive(0)

        @pl.when(s == 4)
        def _():
            all_passed()
            receive(1)

        @pl.when(s == 6)
        def _():
            for way in range(2):
                onward(0, way).wait_recv()

        @pl.when(s == 7)
        def _():
            for way in range(2):
                onward(1, way).wait_recv()

        @pl.when(first)
        def _():
            project(unit)

        @pl.when(jnp.logical_not(first))
        def _():
            finish(unit)

        @pl.when(jnp.logical_not(first) & (unit < 3))
        def _():
            give_back(unit)

        return carry

    lax.fori_loop(0, 8, step, 0)

    def copy(source, target, at, to):
        return send(source, target, send_sem.at[at], recv_sem.at[at], to)

    def far(t):
        k = t // 2
        return t % 2, (2 + k + (k // 2) * (1 + 2 * (k % 2))) % 4

    def trades(t):
        return (
            copy(send_a.at[t % 2], got_a.at[t % 4], 2 * t, peer(0, 0, 1)),
            copy(send_b.at[t % 2], got_b.at[t % 4], 2 * t + 1, peer(0, 0, 1)),
        )

    def forward_a(t, dz, way):
        piece = keep_a.at[t, 1, pl.ds(way * half, half)]
        return copy(piece, fwd_a.at[way, dz], FORWARD_A + 2 * dz + way, peer(1 + 2 * way, 0, 0))

    def full_of_a(t, dz, way):
        return copy(keep_a.at[t, way], full_a.at[way, dz], FULL_A + 2 * dz + way, peer(1 + 2 * way, 0, 0))

    def forward_b(t, dx, hi, way):
        piece = keep_b.at[t, hi, pl.ds(way * half, half)]
        return copy(piece, fwd_b.at[way, dx], FORWARD_B + 2 * dx + way, peer(0, 1 + 2 * way, 0))

    def full_of_b(t, dx, hi, way):
        return copy(keep_b.at[t, hi], full_b.at[way, dx], FULL_B + 2 * dx + way, peer(0, 1 + 2 * way, 0))

    def compute(t):
        p, dz = far(t)
        start = ((x + p) % 4) // 2
        off = 4 * rows * (((dp + p) % 2) * 4 + (z + dz) % 4)
        columns = pl.ds(pl.multiple_of(off, 128), 4 * rows)

        @pl.when(t >= 2)
        def _():
            for trade in trades(t - 2):
                trade.wait_send()

        def put(send_ref, keep_ref, low, total):
            high = low + total.shape[1]
            for hi in range(2):
                spot = (hi + 2 - start) % 2
                even = total[2 * hi * rows : (2 * hi + 1) * rows]
                odd = total[(2 * hi + 1) * rows : (2 * hi + 2) * rows]

                @pl.when(core == 0)
                def _():
                    keep_ref[t, spot, :, low:high] = even
                    send_ref[t % 2, spot, :, low:high] = odd

                @pl.when(core == 1)
                def _():
                    keep_ref[t, spot, :, low:high] = odd
                    send_ref[t % 2, spot, :, low:high] = even

        source = x_all[:, columns]
        put(send_a, keep_a, 0, tn(source, d_all[:, : 2 * width]))
        put(send_b, keep_b, 0, tn(source, d_all[:, 2 * width :]))
        put(send_b, keep_b, width, tn(u_all[:, columns], t_all[...]))
        for trade in trades(t):
            trade.start()

    def pair_up(t):
        p, dz = far(t)
        for trade in trades(t):
            trade.wait_recv()
        keep_a[t] += got_a[t % 4]
        keep_b[t] += got_b[t % 4]

        @pl.when(p == 0)
        def _():
            for way in range(2):
                forward_a(t, dz, way).start()

        @pl.when(dz == 2)
        def _():
            for hi in range(2):
                for way in range(2):
                    forward_b(t, p + 2 * hi, hi, way).start()

    def pass_on(t):
        p, dz = far(t)

        @pl.when(p == 1)
        def _():
            for way in range(2):
                forward_a(t, dz, way).wait_recv()
                keep_a[t, way, pl.ds(way * half, half)] += fwd_a[way, dz]
                full_of_a(t, dz, way).start()

        @pl.when(dz % 2 == 1)
        def _():
            way = dz // 2
            for hi in range(2):
                dx = p + 2 * hi
                forward_b(t, dx, hi, way).wait_recv()
                part = pl.ds(pl.multiple_of(way * half, half), half)
                keep_b[t, hi, part] += fwd_b[way, dx]
                full_of_b(t, dx, hi, way).start()

    def work(t, carry):
        @pl.when(t == 1)
        def _():
            give_back(3)

        @pl.when(t < 8)
        def _():
            compute(t)

        @pl.when((t >= 1) & (t < 9))
        def _():
            pair_up(t - 1)

        @pl.when(t >= 2)
        def _():
            pass_on(t - 2)

        return carry

    lax.fori_loop(0, 10, work, 0)

    def finish_a(dz):
        t = 2 * RANK[dz]
        for way in range(2):
            full_of_a(t, dz, way).wait_recv()
        keep_a[t, 0] += full_a[0, dz] + full_a[1, dz]

    def finish_b(dx):
        t, hi = 6 + dx % 2, dx // 2
        for way in range(2):
            full_of_b(t, dx, hi, way).wait_recv()
        keep_b[t, hi] += full_b[0, dx] + full_b[1, dx]

    def last_of_a(dz):
        return copy(keep_a.at[2 * RANK[dz], 0], last_a.at[dz - 1], LAST_A + dz - 1, peer(0, dz, 0))

    def last_of_b(dx):
        return copy(keep_b.at[6 + dx % 2, dx // 2], last_b.at[dx - 1], LAST_B + dx - 1, peer(dx, 0, 0))

    for d in (2, 3, 1):
        finish_a(d)
        last_of_a(d).start()
        finish_b(d)
        last_of_b(d).start()
    finish_a(0)
    finish_b(0)
    quarter(0)
    quarter(1)
    quarter(2)
    for d in (2, 3, 1):
        last_of_a(d).wait_recv()
        last_of_b(d).wait_recv()
    sum_a = keep_a[6, 0] + last_a[0] + last_a[1] + last_a[2]
    sum_b = keep_b[6, 0] + last_b[0] + last_b[1] + last_b[2]
    qkv_ref[0] = sum_a[:, :width]
    qkv_ref[1] = sum_a[:, width:]
    qkv_ref[2] = sum_b[:, :width]
    proj_ref[...] = sum_b[:, width:]
    quarter(3)

    def settle(frame, carry):
        @pl.when(frame == ctx)
        def _():
            kept().wait()

        @pl.when(frame != ctx)
        def _():
            outward(frame).wait_send()
            inward(frame).wait_recv()

        return carry

    lax.fori_loop(0, n_ctx, settle, 0)

    def home(q, carry):
        for which in range(3):
            back(q, which).wait_send()
        return carry

    lax.fori_loop(0, 4, home, 0)
    for a in range(2):

        def sent(r, carry, a=a):
            swap(a, r).wait_send()
            return carry

        lax.fori_loop(1, n_ctx, sent, 0)
        for way in range(2):
            for h in range(2):
                near(a, h, way).wait_send()
            onward(a, way).wait_send()
    for way in range(2):
        ahead_of_all(way).wait_send()

        def gone(r, carry, way=way):
            passing(way, r).wait_send()
            return carry

        lax.fori_loop(1, n_ctx, gone, 0)
    for t in (6, 7):
        for trade in trades(t):
            trade.wait_send()

    def drain(t, carry):
        p, dz = far(t)

        @pl.when(p == 0)
        def _():
            for way in range(2):
                forward_a(t, dz, way).wait_send()

        @pl.when(p == 1)
        def _():
            for way in range(2):
                full_of_a(t, dz, way).wait_send()

        @pl.when(dz == 2)
        def _():
            for hi in range(2):
                for way in range(2):
                    forward_b(t, p + 2 * hi, hi, way).wait_send()

        @pl.when(dz % 2 == 1)
        def _():
            for hi in range(2):
                full_of_b(t, p + 2 * hi, hi, dz // 2).wait_send()

        return carry

    lax.fori_loop(0, 8, drain, 0)
    for d in (2, 3, 1):
        last_of_a(d).wait_send()
        last_of_b(d).wait_send()


def whole(n_ctx, n_space, rows, inputs, upstream, qkv_weight, out_weight):
    tokens, model = inputs.shape
    width = out_weight.shape[1]
    wide = 2 * width
    vmem, dma = pltpu.VMEM, pltpu.SemaphoreType.DMA
    return pl.pallas_call(
        lambda *refs: whole_kernel(n_ctx, n_space, rows, *refs),
        out_shape=(
            jax.ShapeDtypeStruct((tokens, model), BF16),
            jax.ShapeDtypeStruct((3, rows, width), F32),
            jax.ShapeDtypeStruct((rows, width), F32),
        ),
        in_specs=[pl.BlockSpec(memory_space=pl.ANY)] * 4,
        out_specs=(pl.BlockSpec(memory_space=pl.ANY),) + (pl.BlockSpec(memory_space=vmem),) * 2,
        scratch_shapes=[
            vmem((4 * tokens, model), BF16),
            vmem((4 * tokens, model), BF16),
            vmem((4, model, width), BF16),
            vmem((2, 3, tokens, width), BF16),
            vmem((4 * tokens, 3 * width), BF16),
            vmem((4 * tokens, width), BF16),
            vmem((4, tokens, model), BF16),
            vmem((3, tokens, model), BF16),
            vmem((2, tokens, model * 13 // 24), BF16),
            vmem((8, 2, rows, wide), F32),
            vmem((8, 2, rows, wide), F32),
            vmem((2, 2, rows, wide), F32),
            vmem((2, 2, rows, wide), F32),
            vmem((4, 2, rows, wide), F32),
            vmem((4, 2, rows, wide), F32),
            vmem((2, 4, rows // 2, wide), F32),
            vmem((2, 4, rows // 2, wide), F32),
            vmem((2, 4, rows, wide), F32),
            vmem((2, 4, rows, wide), F32),
            vmem((3, rows, wide), F32),
            vmem((3, rows, wide), F32),
            dma((7,)),
            dma((2, n_ctx)),
            dma((2, n_ctx)),
            dma((12,)),
            dma((12,)),
            dma((COPIES,)),
            dma((COPIES,)),
            dma((4, 3)),
            dma((4, 3)),
            dma((n_ctx,)),
            dma((n_ctx,)),
            dma((2,)),
            dma((2,)),
            dma((2, n_ctx)),
            dma((2, n_ctx)),
        ],
        compiler_params=pltpu.CompilerParams(
            collective_id=0, has_side_effects=True, vmem_limit_bytes=67043328
        ),
        name="whole",
    )(inputs, upstream, qkv_weight, out_weight)


def solution(mesh):
    n_dp, n_ctx, n_space = mesh.shape["dp"], mesh.shape["ctx"], mesh.shape["space"]

    def body(inputs, upstream, qkv_weight, out_weight):
        clips, single, patches, model = inputs.shape
        tokens = clips * patches
        input_grad, qkv_grad, proj_grad = whole(
            n_ctx,
            n_space,
            model // (n_dp * n_ctx),
            inputs.reshape(tokens, model),
            upstream.reshape(tokens, model),
            qkv_weight,
            out_weight,
        )
        return input_grad.reshape(clips, single, patches, model), qkv_grad, proj_grad

    placed = (
        P("dp", "ctx", "space", None),
        P("dp", "ctx", "space", None),
        P(None, None, "space"),
        P(None, "space"),
    )
    return jax.shard_map(
        body,
        mesh=mesh,
        in_specs=placed,
        out_specs=(
            P("dp", "ctx", "space", None),
            P(None, ("dp", "ctx"), "space"),
            P(("dp", "ctx"), "space"),
        ),
        check_vma=False,
    )
```
